32 devices in a mesh: scan: 16 (over z, y, x), col: 2 (over core).
Axes of the slice: x: 2, y: 2, z: 4, core: 2. Of those that a mesh axis runs over, the one named last changes fastest.
Arguments:
- frames: float32 [256, 128, 2048], P('scan', None, 'col'), may hold values from -6 to 6
- depth_offset: int32 [128], replicated, may hold values from -64 to 64
- band_width: int32 [128], replicated, may hold values from 1 to 8
- edge_level: int32 [128, 2048], P(None, 'col'), may hold values from 1 to 16
Outputs:
- volume: float32 [256, 128, 2048], P('scan', None, 'col')
The draws below stay inside these ranges and needn't reach their ends.
All inputs are finite; a program needn't handle non-finite values.
Results may differ from the reference program's by a relative error of at most 0.0003.
Values sent between devices are 32-bit elements; how exact they have to be, the bound alone decides.
A program may use at most 128 MiB of HBM per device.

```python
import jax
import jax.numpy as jnp
from jax import lax

R = 128
C = 2048
BAND = 8
SWEEPS = 6
DIFFUSE = 6
W = 256
SHIFT = 64


def with_ends(values, rng, smallest, largest):
    index_at = [jax.random.randint(jax.random.fold_in(rng, axis), (), 0, length) for axis, length in enumerate(values.shape)]
    widest = values.shape.index(max(values.shape))
    beside = index_at[:widest] + [(index_at[widest] + 1) % values.shape[widest]] + index_at[widest + 1:]
    return values.at[tuple(index_at)].set(smallest).at[tuple(beside)].set(largest)


def level_of(key, dims, cuts, low, high):
    def one(axis_at, parts):
        heights = jax.random.uniform(jax.random.fold_in(jax.random.fold_in(key, 6), axis_at), (parts,), jnp.float32, low / len(cuts), high / len(cuts))
        return jnp.repeat(jnp.exp(heights), dims[axis_at] // parts).reshape((-1,) + (1,) * (len(dims) - axis_at - 1))

    gain = one(*cuts[0])
    for cut in cuts[1:]:
        gain = gain * one(*cut)
    return gain


def gaussian(key, extent, deviation, limit, cuts=(), kind=jnp.bfloat16):
    factor_of = level_of(key, extent, cuts, -0.22, 0.18) if cuts else 1.0
    drawn = jax.random.normal(key, extent, jnp.float32) * deviation * factor_of
    return jnp.minimum(jnp.maximum(drawn, -limit), limit).astype(kind)


def setup_inputs(seed: int = 0) -> dict:
    key_of = jax.random.split(jax.random.key(seed), 5)
    return {
        "frames": gaussian(key_of[0], (W, R, C), 1.0, 6.0, ((0, 16), (2, 2)), jnp.float32),
        "depth_offset": with_ends(jax.random.randint(key_of[1], (R,), 0 - SHIFT, SHIFT + 1), jax.random.fold_in(key_of[1], 1), 0 - SHIFT, SHIFT).astype(jnp.int32),
        "band_width": with_ends(jax.random.randint(key_of[2], (R,), 1, BAND + 1), jax.random.fold_in(key_of[2], 1), 1, BAND).astype(jnp.int32),
        "edge_level": with_ends(jax.random.randint(key_of[3], (R, C), 1, 17), jax.random.fold_in(key_of[3], 1), 1, 16).astype(jnp.int32),
    }


TEMPORAL_KAPPA = 1.0
STEP_SIZE = 0.24
LEVEL_SCALE = 16.0


def diffuse_once(field, kappa, live_mask):
    change = (field[1:] - field[:-1]) * (live_mask[1:] * live_mask[:-1])
    flux_out = change / (1.0 + (change * change) / (kappa * kappa))
    zero_row = jnp.zeros_like(flux_out[:1])
    return field + STEP_SIZE * (jnp.concatenate([flux_out, zero_row], 0) - jnp.concatenate([zero_row, flux_out], 0))


def reference(frames, depth_offset, band_width, edge_level):
    def one_row(row_index):
        plane_rows = lax.dynamic_index_in_dim(frames, row_index, 1, keepdims=False)
        live_mask = jnp.ones((W, 1), jnp.float32)
        for sweep_no in range(SWEEPS):
            plane_rows = diffuse_once(plane_rows, TEMPORAL_KAPPA, live_mask)
        wire_signal = jnp.concatenate([plane_rows[:-1] - plane_rows[1:], jnp.zeros_like(plane_rows[:1])], 0)
        row_offset = lax.dynamic_index_in_dim(depth_offset, row_index, 0, keepdims=False)
        row_width = lax.dynamic_index_in_dim(band_width, row_index, 0, keepdims=False)
        padded = jnp.pad(wire_signal, ((SHIFT + BAND, SHIFT), (0, 0)))
        summed = jnp.zeros_like(wire_signal)
        for lag_step in range(BAND):
            start_at = (SHIFT + BAND - lag_step - row_offset).astype(jnp.int32)
            pieces = lax.dynamic_slice_in_dim(padded, start_at, W, 0)
            summed = summed + jnp.where(lag_step < row_width, pieces, jnp.zeros_like(pieces))
        profile = summed / row_width.astype(jnp.float32)
        edge_scale = lax.dynamic_index_in_dim(edge_level, row_index, 0, keepdims=True).astype(jnp.float32) / LEVEL_SCALE
        for sweep_no in range(DIFFUSE):
            profile = diffuse_once(profile, edge_scale, live_mask)
        return profile

    stacked = lax.map(one_row, jnp.arange(R, dtype=jnp.int32))
    return jnp.transpose(stacked, (1, 0, 2))
```

```python
import functools

import jax
import jax.numpy as jnp
from jax import lax
from jax.experimental import pallas as pl
from jax.experimental.pallas import tpu as pltpu
from jax.sharding import PartitionSpec as P

SWEEPS = 6
DIFFUSE = 6
BAND = 8
STEP_SIZE = 0.24
LEVEL_SCALE = 16.0
LANES = 128
ROWS = 8
LEAD = 4
LAG = 2
SLOTS = 3
UNROLL = 4
LO = DIFFUSE + BAND - 1
MESH = pl.DeviceIdType.MESH
RATE = 1.0 / STEP_SIZE
UNIT = STEP_SIZE**0.5


def after(block):
    least = DIFFUSE + 1
    return least + -(LO + block + least) % ROWS


def lengths(offset, block):
    beyond = -offset + (DIFFUSE + 1 - after(block))
    up = (jnp.maximum(offset, 0) + ROWS - 1) // ROWS
    down = (jnp.maximum(beyond, 0) + ROWS - 1) // ROWS
    return up, down


def sweep_pass(load, store, n_in, n_out, sweeps, streams):
    lead = (n_in - n_out) // 2 + 2 * sweeps - 1

    def advance(t, carry):
        held, flux, made = carry
        at = jnp.minimum(t, n_in - 1)
        new_held, new_flux, new_made = [], [], []
        for s in range(streams):
            fresh = load(at, s)
            for level in range(sweeps):
                k = s * sweeps + level
                b = fresh if level == 0 else made[k - 1]
                a = held[k]
                c = b - a
                d = RATE + c * c
                q = pl.reciprocal(d, approx=True)
                f = c * (q * (2.0 - d * q))
                new_made.append(a + (f - flux[k]))
                new_held.append(b)
                new_flux.append(f)
        return tuple(new_held), tuple(new_flux), tuple(new_made)

    def work(t, carry):
        carry = advance(t + lead, carry)
        for s in range(streams):
            store(t, s, carry[2][s * sweeps + sweeps - 1])
        return carry

    start = tuple(load(0, s) for s in range(streams) for _ in range(sweeps))
    carry = lax.fori_loop(0, lead, advance, (start, start, start))
    lax.fori_loop(0, n_out, work, carry, unroll=UNROLL)


def kernel(group, chunks, room, off_ref, bw_ref, x, edge, out, *scratch):
    from_up = scratch[:chunks]
    from_down = scratch[chunks : 2 * chunks]
    wins = scratch[2 * chunks : 2 * chunks + SLOTS]
    (raw, made, prof, gain, pack_up, pack_down, edge_v, len_up, len_down, next_up, next_down, base_up, base_down,
     slot_up, slot_down, in_send, in_recv, in_own, halo_send, halo_recv, far_send, far_recv, out_send,
     out_recv, out_own, edge_sem) = scratch[2 * chunks + SLOTS :]
    local = x.shape[0]
    rows = x.shape[1] // group
    block = local * group
    hi = after(block)
    own_at = block + LO
    raw_at = LO + SWEEPS
    n_raw = raw.shape[1]
    ext = LO + block + hi
    spans = block // ROWS
    reach = 2 * block + ext
    me = lax.axis_index("scan")
    k = lax.rem(me, group)
    z = lax.div(me, group)
    tile_count = rows // ROWS
    pair = 2 if tile_count % 2 == 0 else 1

    def rows_of(j):
        return pl.ds(pl.multiple_of(j * rows, ROWS), rows)

    def cols_of(c):
        return pl.ds(c * LANES, LANES)

    def mate(m):
        return z * group + lax.rem(k + m, group)

    has = {1: z < LEAD - 1, -1: z > 0}
    gets = {1: z > 0, -1: z < LEAD - 1}

    barrier = pltpu.get_barrier_semaphore()
    for m in range(1, group):
        pl.semaphore_signal(barrier, inc=1, device_id={"scan": mate(m)}, device_id_type=MESH)
    for step in (1, -1):

        @pl.when(has[step])
        def _(step=step):
            pl.semaphore_signal(
                barrier, inc=1, device_id={"scan": me + step * group}, device_id_type=MESH
            )

    count = group - 1
    for step in (1, -1):
        count = count + has[step].astype(jnp.int32)
    pl.semaphore_wait(barrier, count)

    def in_copy(c, m):
        return pltpu.make_async_remote_copy(
            src_ref=x.at[:, rows_of(lax.rem(k + m, group)), cols_of(c)],
            dst_ref=raw.at[c, pl.ds(raw_at + k * local, local)],
            send_sem=in_send.at[c, m - 1],
            recv_sem=in_recv.at[c, m - 1],
            device_id={"scan": mate(m)},
            device_id_type=MESH,
        )

    def in_local(c):
        return pltpu.make_async_copy(
            x.at[:, rows_of(k), cols_of(c)],
            raw.at[c, pl.ds(raw_at + k * local, local)],
            in_own.at[c],
        )

    def out_copy(c, m):
        return pltpu.make_async_remote_copy(
            src_ref=made.at[c, pl.ds(lax.rem(k + m, group) * local, local)],
            dst_ref=out.at[:, rows_of(k), cols_of(c)],
            send_sem=out_send.at[c, m - 1],
            recv_sem=out_recv.at[c, m - 1],
            device_id={"scan": mate(m)},
            device_id_type=MESH,
        )

    def out_local(c):
        return pltpu.make_async_copy(
            made.at[c, pl.ds(k * local, local)],
            out.at[:, rows_of(k), cols_of(c)],
            out_own.at[c],
        )

    def z_copy(src, dst, sems, c, i, step):
        send, recv = sems
        return pltpu.make_async_remote_copy(
            src_ref=src,
            dst_ref=dst,
            send_sem=send.at[c, i],
            recv_sem=recv.at[c, i],
            device_id={"scan": me + step * group},
            device_id_type=MESH,
        )

    def halo_copies(c):
        sems = (halo_send, halo_recv)
        up = z_copy(
            raw.at[c, pl.ds(block, raw_at)], raw.at[c, pl.ds(0, raw_at)], sems, c, 0, 1
        )
        down = z_copy(
            raw.at[c, pl.ds(raw_at, hi + SWEEPS)],
            raw.at[c, pl.ds(raw_at + block, hi + SWEEPS)], sems, c, 1, -1,
        )
        return ((1, up), (-1, down))

    def far_copies(c):
        sems = (far_send, far_recv)
        up = z_copy(
            pack_up.at[c % SLOTS], from_up[c].at[pl.ds(spans, room)], sems, c, 0, 1
        )
        down = z_copy(
            pack_down.at[c % SLOTS], from_down[c].at[pl.ds(0, room)], sems, c, 1, -1
        )
        return ((1, up), (-1, down))

    def start(copies):
        for step, copy in copies:
            pl.when(has[step])(copy.start)

    def wait_recv(copies):
        for step, copy in copies:
            pl.when(gets[step])(copy.wait_recv)

    def wait_send(copies):
        for step, copy in copies:
            pl.when(has[step])(copy.wait_send)

    edge_copy = pltpu.make_async_copy(edge.at[rows_of(k)], edge_v, edge_sem)
    for c in range(chunks):
        for m in range(1, group):
            in_copy(c, m).start()
        in_local(c).start()
    edge_copy.start()

    for lens, nexts, bases in ((len_up, next_up, base_up), (len_down, next_down, base_down)):
        lens[rows] = jnp.int32(1)
        nexts[rows] = jnp.int32(rows)

    def measure(r, base):
        up, down = lengths(off_ref[k * rows + r], block)
        len_up[r], len_down[r] = up, down
        base_up[r], base_down[r] = base[0] + up, base[1]
        return base[0] + up, base[1] + down

    lax.fori_loop(0, rows, measure, (jnp.int32(0), jnp.int32(0)))

    def link(i, _):
        r = rows - 1 - i
        for lens, nexts in ((len_up, next_up), (len_down, next_down)):
            nexts[r] = jnp.where(lens[r + 1] > 0, r + 1, nexts[r + 1])
        return 0

    lax.fori_loop(0, rows, link, 0)

    def assign(j, carry):
        result = []
        lists = ((len_up, next_up, slot_up, own_at + block - LO), (len_down, next_down, slot_down, own_at + hi))
        for i, (lens, nexts, slots, first) in enumerate(lists):
            row, p = carry[2 * i], carry[2 * i + 1]
            n = lens[row]
            frame = first + ROWS * p - (ROWS * n if i == 0 else 0)
            slots[j] = jnp.where(row < rows, row * reach + frame, own_at)
            done = p + 1 >= n
            result.append(jnp.where(done, nexts[row], row))
            result.append(jnp.where(done, 0, p + 1))
        return tuple(result)

    heads = []
    for lens, nexts in ((len_up, next_up), (len_down, next_down)):
        heads.append(jnp.where(lens[0] > 0, 0, nexts[0]))
        heads.append(jnp.int32(0))
    lax.fori_loop(0, room, assign, tuple(heads))

    def arrive(c):
        in_local(c).wait()
        for m in range(1, group):
            in_copy(c, m).wait_recv()
        start(halo_copies(c))

    def across(win, tile, frame):
        return win.at[pl.ds(tile * (ROWS * reach) + frame, ROWS, stride=reach)]

    def smooth(c):
        win = wins[c % SLOTS]
        wait_recv(halo_copies(c))

        @pl.when(z == 0)
        def _():
            for i in range(raw_at):
                raw[c, raw_at - 1 - i] = raw[c, raw_at + i]

        @pl.when(z == LEAD - 1)
        def _():
            for i in range(hi + SWEEPS):
                raw[c, raw_at + block + i] = raw[c, raw_at + block - 1 - i]

        def one(p, _):
            def load(t, s):
                at = pl.ds(pl.multiple_of((p * pair + s) * ROWS, ROWS), ROWS)
                return raw[c, t, at, :] * (1.0 / UNIT)

            def store(t, s, value):
                across(win, p * pair + s, block + t)[...] = value

            sweep_pass(load, store, n_raw, ext, SWEEPS, pair)
            return 0

        lax.fori_loop(0, tile_count // pair, one, 0)

        def repeat(first, number, source):
            values = [across(win, p, source)[...] for p in range(tile_count)]

            def one(i, _):
                for p in range(tile_count):
                    across(win, p, first + i)[...] = values[p]
                return 0

            lax.fori_loop(0, number, one, 0)

        pl.when(z == 0)(lambda: repeat(0, own_at, own_at))
        pl.when(z == LEAD - 1)(lambda: repeat(own_at + block, hi + block, own_at + block - 1))
        if c >= SLOTS:
            wait_send(far_copies(c - SLOTS))

        def pack(j, _):
            for slots, packed in ((slot_up, pack_up), (slot_down, pack_down)):
                packed[c % SLOTS, j] = win[pl.ds(slots[j], ROWS), :]
            return 0

        lax.fori_loop(0, room, pack, 0, unroll=4)
        start(far_copies(c))

    def unpack(win, source, bases, first):
        def one(r, _):
            base = bases[r]
            for m in range(spans):
                to = pl.multiple_of(r * reach + first + ROWS * m, ROWS)
                win[pl.ds(to, ROWS), :] = source[base + m]
            return 0

        lax.fori_loop(0, rows, one, 0)

    def depth(c):
        win = wins[c % SLOTS]
        wait_recv(far_copies(c))
        pl.when(gets[1])(lambda: unpack(win, from_up[c], base_up, 0))
        pl.when(gets[-1])(lambda: unpack(win, from_down[c], base_down, own_at + block + hi))

        for p in range(tile_count):
            tile = pl.ds(p * ROWS, ROWS)
            gain[tile, :] = LEVEL_SCALE / edge_v[tile, pl.ds(c * LANES, LANES)].astype(jnp.float32)

        def fill(r, _):
            width = bw_ref[k * rows + r]
            at_b = r * reach + own_at - DIFFUSE + 1 - off_ref[k * rows + r]
            at_a = at_b - width
            scale = jnp.broadcast_to(gain[pl.ds(r, 1), :], (ROWS, LANES)) / width.astype(jnp.float32)
            for m in range(prof.shape[0] // (rows * ROWS)):
                a = win[pl.ds(at_a + m * ROWS, ROWS), :]
                b = win[pl.ds(at_b + m * ROWS, ROWS), :]
                prof[pl.ds(m * ROWS * rows + r, ROWS, stride=rows), :] = (a - b) * scale
            return 0

        lax.fori_loop(0, rows, fill, 0)

        def bins(d):
            return pl.ds(d * rows, rows)

        @pl.when(z == 0)
        def _():
            for i in range(DIFFUSE):
                prof[bins(DIFFUSE - 1 - i), :] = prof[bins(DIFFUSE + i), :]

        @pl.when(z == LEAD - 1)
        def _():
            for i in range(DIFFUSE):
                prof[bins(DIFFUSE + block + i), :] = prof[bins(DIFFUSE + block - 1 - i), :]

        def one(p, _):
            tiles = [pl.ds(pl.multiple_of((p * pair + s) * ROWS, ROWS), ROWS) for s in range(pair)]
            scales = [
                edge_v[tile, pl.ds(c * LANES, LANES)].astype(jnp.float32) * (UNIT / LEVEL_SCALE) for tile in tiles
            ]

            def load(t, s):
                return prof[pl.ds(pl.multiple_of(t * rows + (p * pair + s) * ROWS, ROWS), ROWS), :]

            def store(t, s, value):
                made[c, t, tiles[s], :] = value * scales[s]

            sweep_pass(load, store, block + 2 * DIFFUSE, block, DIFFUSE, pair)
            return 0

        lax.fori_loop(0, tile_count // pair, one, 0)
        for m in range(1, group):
            out_copy(c, m).start()
        out_local(c).start()

    arrive(0)
    for c in range(chunks):
        if c + 1 < chunks:
            arrive(c + 1)
        smooth(c)
        if c == 0:
            edge_copy.wait()
        if c >= LAG:
            depth(c - LAG)
    for c in range(max(chunks - LAG, 0), chunks):
        depth(c)
    for c in range(chunks):
        for m in range(1, group):
            in_copy(c, m).wait_send()
        wait_send(halo_copies(c))
        if c >= chunks - SLOTS:
            wait_send(far_copies(c))
        out_local(c).wait()
        for m in range(1, group):
            out_copy(c, m).wait()


def body(frames, depth_offset, band_width, edge_level):
    group = lax.axis_size("scan") // LEAD
    local, all_rows, cols = frames.shape
    chunks, rows, block = cols // LANES, all_rows // group, local * group
    hi, spans = after(block), block // ROWS
    bins = -(-(block + 2 * DIFFUSE) // ROWS) * ROWS
    dma = pltpu.SemaphoreType.DMA
    smem = pl.BlockSpec(memory_space=pltpu.SMEM)
    anywhere = pl.BlockSpec(memory_space=pl.ANY)

    def vmem(*shape):
        return pltpu.VMEM(shape, jnp.float32)

    def table(size):
        return pltpu.SMEM((size,), jnp.int32)

    def with_room(room, call):
        arrived = vmem(spans + room, ROWS, LANES)
        packed = vmem(SLOTS, room, ROWS, LANES)
        return pl.pallas_call(
            functools.partial(kernel, group, chunks, room),
            out_shape=jax.ShapeDtypeStruct(frames.shape, frames.dtype),
            in_specs=[smem, smem, anywhere, anywhere],
            out_specs=anywhere,
            scratch_shapes=[arrived] * (2 * chunks)
            + [vmem((3 * block + LO + hi) * rows, LANES)] * SLOTS
            + [
                vmem(chunks, LO + block + hi + 2 * SWEEPS, rows, LANES),
                vmem(chunks, block, rows, LANES),
                vmem(bins * rows, LANES),
                vmem(rows, LANES),
                packed,
                packed,
                pltpu.VMEM((rows, cols), jnp.int32),
            ]
            + [table(rows + 1)] * 6
            + [table(room)] * 2
            + [
                dma((chunks, group - 1)),
                dma((chunks, group - 1)),
                dma((chunks,)),
                dma((chunks, 2)),
                dma((chunks, 2)),
                dma((chunks, 2)),
                dma((chunks, 2)),
                dma((chunks, group - 1)),
                dma((chunks, group - 1)),
                dma((chunks,)),
                dma,
            ],
            compiler_params=pltpu.CompilerParams(
                collective_id=call, has_side_effects=True, vmem_limit_bytes=60 * 1024 * 1024
            ),
        )

    whole = rows * spans
    half = whole // 2
    taken = [jnp.max(jnp.sum(n.reshape(group, rows), 1)) for n in lengths(depth_offset, block)]
    fits = jnp.maximum(*taken) <= half
    return lax.cond(
        fits, with_room(half, 0), with_room(whole, 1), depth_offset, band_width, frames, edge_level
    )


def solution(mesh):
    placed = (P("scan", None, "col"), P(), P(), P(None, "col"))
    return jax.shard_map(
        body, mesh=mesh, in_specs=placed, out_specs=P("scan", None, "col"), check_vma=False
    )
```

```python
import functools

import jax
import jax.numpy as jnp
from jax import lax
from jax.experimental import pallas as pl
from jax.experimental.pallas import tpu as pltpu
from jax.sharding import PartitionSpec as P

SWEEPS = 6
DIFFUSE = 6
BAND = 8
STEP_SIZE = 0.24
LEVEL_SCALE = 16.0
LANES = 128
ROWS = 8
LEAD = 4
LAG = 1
SLOTS = 3
UNROLL = 4
LO = DIFFUSE + BAND - 1
MESH = pl.DeviceIdType.MESH
RATE = 1.0 / STEP_SIZE
UNIT = STEP_SIZE**0.5


def after(block):
    least = DIFFUSE + 1
    return least + -(LO + block + least) % ROWS


def lengths(offset, block):
    beyond = -offset + (DIFFUSE + 1 - after(block))
    up = (jnp.maximum(offset, 0) + ROWS - 1) // ROWS
    down = (jnp.maximum(beyond, 0) + ROWS - 1) // ROWS
    return up, down


def sweep_pass(load, store, n_in, n_out, sweeps, streams):
    lead = (n_in - n_out) // 2 + 2 * sweeps - 1

    def advance(t, carry):
        held, flux, made = carry
        at = jnp.minimum(t, n_in - 1)
        new_held, new_flux, new_made = [], [], []
        for s in range(streams):
            fresh = load(at, s)
            for level in range(sweeps):
                k = s * sweeps + level
                b = fresh if level == 0 else made[k - 1]
                a = held[k]
                c = b - a
                d = RATE + c * c
                q = pl.reciprocal(d, approx=True)
                f = c * (q * (2.0 - d * q))
                new_made.append(a + (f - flux[k]))
                new_held.append(b)
                new_flux.append(f)
        return tuple(new_held), tuple(new_flux), tuple(new_made)

    def work(t, carry):
        carry = advance(t + lead, carry)
        for s in range(streams):
            store(t, s, carry[2][s * sweeps + sweeps - 1])
        return carry

    start = tuple(load(0, s) for s in range(streams) for _ in range(sweeps))
    carry = lax.fori_loop(0, lead, advance, (start, start, start))
    lax.fori_loop(0, n_out, work, carry, unroll=UNROLL)


def kernel(group, chunks, room, off_ref, bw_ref, x, edge, out, *scratch):
    from_up = scratch[:chunks]
    from_down = scratch[chunks : 2 * chunks]
    wins = scratch[2 * chunks : 2 * chunks + SLOTS]
    (raw, made, prof, gain, pack_up, pack_down, edge_v, len_up, len_down, next_up, next_down, base_up, base_down,
     slot_up, slot_down, in_send, in_recv, in_own, halo_send, halo_recv, far_send, far_recv, out_send,
     out_recv, out_own, edge_sem) = scratch[2 * chunks + SLOTS :]
    local = x.shape[0]
    rows = x.shape[1] // group
    block = local * group
    hi = after(block)
    own_at = block + LO
    raw_at = LO + SWEEPS
    n_raw = raw.shape[1]
    ext = LO + block + hi
    spans = block // ROWS
    reach = 2 * block + ext
    me = lax.axis_index("scan")
    k = lax.rem(me, group)
    z = lax.div(me, group)
    tile_count = rows // ROWS
    pair = 2 if tile_count % 2 == 0 else 1

    def rows_of(j):
        return pl.ds(pl.multiple_of(j * rows, ROWS), rows)

    def cols_of(c):
        return pl.ds(c * LANES, LANES)

    def mate(m):
        return z * group + lax.rem(k + m, group)

    has = {1: z < LEAD - 1, -1: z > 0}
    gets = {1: z > 0, -1: z < LEAD - 1}

    barrier = pltpu.get_barrier_semaphore()
    for m in range(1, group):
        pl.semaphore_signal(barrier, inc=1, device_id={"scan": mate(m)}, device_id_type=MESH)
    for step in (1, -1):

        @pl.when(has[step])
        def _(step=step):
            pl.semaphore_signal(
                barrier, inc=1, device_id={"scan": me + step * group}, device_id_type=MESH
            )

    count = group - 1
    for step in (1, -1):
        count = count + has[step].astype(jnp.int32)
    pl.semaphore_wait(barrier, count)

    def in_copy(c, m):
        return pltpu.make_async_remote_copy(
            src_ref=x.at[:, rows_of(lax.rem(k + m, group)), cols_of(c)],
            dst_ref=raw.at[c, pl.ds(raw_at + k * local, local)],
            send_sem=in_send.at[c, m - 1],
            recv_sem=in_recv.at[c, m - 1],
            device_id={"scan": mate(m)},
            device_id_type=MESH,
        )

    def in_local(c):
        return pltpu.make_async_copy(
            x.at[:, rows_of(k), cols_of(c)],
            raw.at[c, pl.ds(raw_at + k * local, local)],
            in_own.at[c],
        )

    def out_copy(c, m):
        return pltpu.make_async_remote_copy(
            src_ref=made.at[c % SLOTS, pl.ds(lax.rem(k + m, group) * local, local)],
            dst_ref=out.at[:, rows_of(k), cols_of(c)],
            send_sem=out_send.at[c, m - 1],
            recv_sem=out_recv.at[c, m - 1],
            device_id={"scan": mate(m)},
            device_id_type=MESH,
        )

    def out_local(c):
        return pltpu.make_async_copy(
            made.at[c % SLOTS, pl.ds(k * local, local)],
            out.at[:, rows_of(k), cols_of(c)],
            out_own.at[c],
        )

    def z_copy(src, dst, sems, c, i, step):
        send, recv = sems
        return pltpu.make_async_remote_copy(
            src_ref=src,
            dst_ref=dst,
            send_sem=send.at[c, i],
            recv_sem=recv.at[c, i],
            device_id={"scan": me + step * group},
            device_id_type=MESH,
        )

    def halo_copies(c):
        sems = (halo_send, halo_recv)
        up = z_copy(
            raw.at[c, pl.ds(block, raw_at)], raw.at[c, pl.ds(0, raw_at)], sems, c, 0, 1
        )
        down = z_copy(
            raw.at[c, pl.ds(raw_at, hi + SWEEPS)],
            raw.at[c, pl.ds(raw_at + block, hi + SWEEPS)], sems, c, 1, -1,
        )
        return ((1, up), (-1, down))

    def far_copies(c):
        sems = (far_send, far_recv)
        up = z_copy(
            pack_up.at[c % SLOTS], from_up[c].at[pl.ds(spans, room)], sems, c, 0, 1
        )
        down = z_copy(
            pack_down.at[c % SLOTS], from_down[c].at[pl.ds(0, room)], sems, c, 1, -1
        )
        return ((1, up), (-1, down))

    def start(copies):
        for step, copy in copies:
            pl.when(has[step])(copy.start)

    def wait_recv(copies):
        for step, copy in copies:
            pl.when(gets[step])(copy.wait_recv)

    def wait_send(copies):
        for step, copy in copies:
            pl.when(has[step])(copy.wait_send)

    edge_copy = pltpu.make_async_copy(edge.at[rows_of(k)], edge_v, edge_sem)
    for c in range(chunks):
        for m in range(1, group):
            in_copy(c, m).start()
        in_local(c).start()
    edge_copy.start()

    for lens, nexts, bases in ((len_up, next_up, base_up), (len_down, next_down, base_down)):
        lens[rows] = jnp.int32(1)
        nexts[rows] = jnp.int32(rows)

    def measure(r, base):
        up, down = lengths(off_ref[k * rows + r], block)
        len_up[r], len_down[r] = up, down
        base_up[r], base_down[r] = base[0] + up, base[1]
        return base[0] + up, base[1] + down

    lax.fori_loop(0, rows, measure, (jnp.int32(0), jnp.int32(0)))

    def link(i, _):
        r = rows - 1 - i
        for lens, nexts in ((len_up, next_up), (len_down, next_down)):
            nexts[r] = jnp.where(lens[r + 1] > 0, r + 1, nexts[r + 1])
        return 0

    lax.fori_loop(0, rows, link, 0)

    def assign(j, carry):
        result = []
        lists = ((len_up, next_up, slot_up, own_at + block - LO), (len_down, next_down, slot_down, own_at + hi))
        for i, (lens, nexts, slots, first) in enumerate(lists):
            row, p = carry[2 * i], carry[2 * i + 1]
            n = lens[row]
            frame = first + ROWS * p - (ROWS * n if i == 0 else 0)
            slots[j] = jnp.where(row < rows, row * reach + frame, own_at)
            done = p + 1 >= n
            result.append(jnp.where(done, nexts[row], row))
            result.append(jnp.where(done, 0, p + 1))
        return tuple(result)

    heads = []
    for lens, nexts in ((len_up, next_up), (len_down, next_down)):
        heads.append(jnp.where(lens[0] > 0, 0, nexts[0]))
        heads.append(jnp.int32(0))
    lax.fori_loop(0, room, assign, tuple(heads))

    def arrive(c):
        in_local(c).wait()
        for m in range(1, group):
            in_copy(c, m).wait_recv()
        start(halo_copies(c))

    def across(win, tile, frame):
        return win.at[pl.ds(tile * (ROWS * reach) + frame, ROWS, stride=reach)]

    def smooth(c):
        win = wins[c % SLOTS]
        wait_recv(halo_copies(c))

        @pl.when(z == 0)
        def _():
            for i in range(raw_at):
                raw[c, raw_at - 1 - i] = raw[c, raw_at + i]

        @pl.when(z == LEAD - 1)
        def _():
            for i in range(hi + SWEEPS):
                raw[c, raw_at + block + i] = raw[c, raw_at + block - 1 - i]

        def one(p, _):
            def load(t, s):
                at = pl.ds(pl.multiple_of((p * pair + s) * ROWS, ROWS), ROWS)
                return raw[c, t, at, :] * (1.0 / UNIT)

            def store(t, s, value):
                across(win, p * pair + s, block + t)[...] = value

            sweep_pass(load, store, n_raw, ext, SWEEPS, pair)
            return 0

        lax.fori_loop(0, tile_count // pair, one, 0)

        def repeat(first, number, source):
            values = [across(win, p, source)[...] for p in range(tile_count)]

            def one(i, _):
                for p in range(tile_count):
                    across(win, p, first + i)[...] = values[p]
                return 0

            lax.fori_loop(0, number, one, 0)

        pl.when(z == 0)(lambda: repeat(0, own_at, own_at))
        pl.when(z == LEAD - 1)(lambda: repeat(own_at + block, hi + block, own_at + block - 1))
        if c >= SLOTS:
            wait_send(far_copies(c - SLOTS))

        def pack(j, _):
            for slots, packed in ((slot_up, pack_up), (slot_down, pack_down)):
                packed[c % SLOTS, j] = win[pl.ds(slots[j], ROWS), :]
            return 0

        lax.fori_loop(0, room, pack, 0, unroll=4)
        start(far_copies(c))

    def unpack(win, source, bases, first):
        def one(r, _):
            base = bases[r]
            for m in range(spans):
                to = pl.multiple_of(r * reach + first + ROWS * m, ROWS)
                win[pl.ds(to, ROWS), :] = source[base + m]
            return 0

        lax.fori_loop(0, rows, one, 0)

    def depth(c):
        win = wins[c % SLOTS]
        wait_recv(far_copies(c))
        pl.when(gets[1])(lambda: unpack(win, from_up[c], base_up, 0))
        pl.when(gets[-1])(lambda: unpack(win, from_down[c], base_down, own_at + block + hi))

        for p in range(tile_count):
            tile = pl.ds(p * ROWS, ROWS)
            gain[tile, :] = LEVEL_SCALE / edge_v[tile, pl.ds(c * LANES, LANES)].astype(jnp.float32)

        def fill(r, _):
            width = bw_ref[k * rows + r]
            at_b = r * reach + own_at - DIFFUSE + 1 - off_ref[k * rows + r]
            at_a = at_b - width
            scale = jnp.broadcast_to(gain[pl.ds(r, 1), :], (ROWS, LANES)) / width.astype(jnp.float32)
            for m in range(prof.shape[0] // (rows * ROWS)):
                a = win[pl.ds(at_a + m * ROWS, ROWS), :]
                b = win[pl.ds(at_b + m * ROWS, ROWS), :]
                prof[pl.ds(m * ROWS * rows + r, ROWS, stride=rows), :] = (a - b) * scale
            return 0

        lax.fori_loop(0, rows, fill, 0)

        def bins(d):
            return pl.ds(d * rows, rows)

        @pl.when(z == 0)
        def _():
            for i in range(DIFFUSE):
                prof[bins(DIFFUSE - 1 - i), :] = prof[bins(DIFFUSE + i), :]

        @pl.when(z == LEAD - 1)
        def _():
            for i in range(DIFFUSE):
                prof[bins(DIFFUSE + block + i), :] = prof[bins(DIFFUSE + block - 1 - i), :]

        def one(p, _):
            tiles = [pl.ds(pl.multiple_of((p * pair + s) * ROWS, ROWS), ROWS) for s in range(pair)]
            scales = [
                edge_v[tile, pl.ds(c * LANES, LANES)].astype(jnp.float32) * (UNIT / LEVEL_SCALE) for tile in tiles
            ]

            def load(t, s):
                return prof[pl.ds(pl.multiple_of(t * rows + (p * pair + s) * ROWS, ROWS), ROWS), :]

            def store(t, s, value):
                made[c % SLOTS, t, tiles[s], :] = value * scales[s]

            sweep_pass(load, store, block + 2 * DIFFUSE, block, DIFFUSE, pair)
            return 0

        if c >= SLOTS:
            sent(c - SLOTS)
        lax.fori_loop(0, tile_count // pair, one, 0)
        for m in range(1, group):
            out_copy(c, m).start()
        out_local(c).start()

    def sent(c):
        out_local(c).wait()
        for m in range(1, group):
            out_copy(c, m).wait_send()

    arrive(0)
    for c in range(chunks):
        if c + 1 < chunks:
            arrive(c + 1)
        smooth(c)
        if c == 0:
            edge_copy.wait()
        if c >= LAG:
            depth(c - LAG)
    for c in range(max(chunks - LAG, 0), chunks):
        depth(c)
    for c in range(chunks):
        for m in range(1, group):
            in_copy(c, m).wait_send()
        wait_send(halo_copies(c))
        if c >= chunks - SLOTS:
            wait_send(far_copies(c))
        if c >= chunks - SLOTS:
            sent(c)
        for m in range(1, group):
            out_copy(c, m).wait_recv()


def body(frames, depth_offset, band_width, edge_level):
    group = lax.axis_size("scan") // LEAD
    local, all_rows, cols = frames.shape
    chunks, rows, block = cols // LANES, all_rows // group, local * group
    hi, spans = after(block), block // ROWS
    bins = -(-(block + 2 * DIFFUSE) // ROWS) * ROWS
    dma = pltpu.SemaphoreType.DMA
    smem = pl.BlockSpec(memory_space=pltpu.SMEM)
    anywhere = pl.BlockSpec(memory_space=pl.ANY)

    def vmem(*shape):
        return pltpu.VMEM(shape, jnp.float32)

    def table(size):
        return pltpu.SMEM((size,), jnp.int32)

    def with_room(room, call):
        arrived = vmem(spans + room, ROWS, LANES)
        packed = vmem(SLOTS, room, ROWS, LANES)
        return pl.pallas_call(
            functools.partial(kernel, group, chunks, room),
            out_shape=jax.ShapeDtypeStruct(frames.shape, frames.dtype),
            in_specs=[smem, smem, anywhere, anywhere],
            out_specs=anywhere,
            scratch_shapes=[arrived] * (2 * chunks)
            + [vmem((3 * block + LO + hi) * rows, LANES)] * SLOTS
            + [
                vmem(chunks, LO + block + hi + 2 * SWEEPS, rows, LANES),
                vmem(SLOTS, block, rows, LANES),
                vmem(bins * rows, LANES),
                vmem(rows, LANES),
                packed,
                packed,
                pltpu.VMEM((rows, cols), jnp.int32),
            ]
            + [table(rows + 1)] * 6
            + [table(room)] * 2
            + [
                dma((chunks, group - 1)),
                dma((chunks, group - 1)),
                dma((chunks,)),
                dma((chunks, 2)),
                dma((chunks, 2)),
                dma((chunks, 2)),
                dma((chunks, 2)),
                dma((chunks, group - 1)),
                dma((chunks, group - 1)),
                dma((chunks,)),
                dma,
            ],
            compiler_params=pltpu.CompilerParams(
                collective_id=call, has_side_effects=True, vmem_limit_bytes=52 * 1024 * 1024
            ),
        )

    whole = rows * spans
    half = whole // 2
    taken = [jnp.max(jnp.sum(n.reshape(group, rows), 1)) for n in lengths(depth_offset, block)]
    fits = jnp.maximum(*taken) <= half
    return lax.cond(
        fits, with_room(half, 0), with_room(whole, 1), depth_offset, band_width, frames, edge_level
    )


def solution(mesh):
    placed = (P("scan", None, "col"), P(), P(), P(None, "col"))
    return jax.shard_map(
        body, mesh=mesh, in_specs=placed, out_specs=P("scan", None, "col"), check_vma=False
    )
```

```python
import functools

import jax
import jax.numpy as jnp
from jax import lax
from jax.experimental import pallas as pl
from jax.experimental.pallas import tpu as pltpu
from jax.sharding import PartitionSpec as P

SWEEPS = 6
DIFFUSE = 6
BAND = 8
STEP_SIZE = 0.24
LEVEL_SCALE = 16.0
LANES = 128
ROWS = 8
LEAD = 4
LAG = 1
SLOTS = 3
UNROLL = 4
LO = DIFFUSE + BAND - 1
MESH = pl.DeviceIdType.MESH
RATE = 1.0 / STEP_SIZE
UNIT = STEP_SIZE**0.5


def after(block):
    least = DIFFUSE + 1
    return least + -(LO + block + least) % ROWS


def lengths(offset, block):
    beyond = -offset + (DIFFUSE + 1 - after(block))
    up = (jnp.maximum(offset, 0) + ROWS - 1) // ROWS
    down = (jnp.maximum(beyond, 0) + ROWS - 1) // ROWS
    return up, down


def sweep_pass(load, store, n_in, n_out, sweeps, streams):
    lead = (n_in - n_out) // 2 + 2 * sweeps - 1

    def advance(t, carry):
        held, flux, made = carry
        at = jnp.minimum(t, n_in - 1)
        new_held, new_flux, new_made = [], [], []
        for s in range(streams):
            fresh = load(at, s)
            for level in range(sweeps):
                k = s * sweeps + level
                b = fresh if level == 0 else made[k - 1]
                a = held[k]
                c = b - a
                d = RATE + c * c
                q = pl.reciprocal(d, approx=True)
                f = c * (q * (2.0 - d * q))
                new_made.append(a + (f - flux[k]))
                new_held.append(b)
                new_flux.append(f)
        return tuple(new_held), tuple(new_flux), tuple(new_made)

    def work(t, carry):
        carry = advance(t + lead, carry)
        for s in range(streams):
            store(t, s, carry[2][s * sweeps + sweeps - 1])
        return carry

    start = tuple(load(0, s) for s in range(streams) for _ in range(sweeps))
    carry = lax.fori_loop(0, lead, advance, (start, start, start))
    lax.fori_loop(0, n_out, work, carry, unroll=UNROLL)


def kernel(group, chunks, room, offsets, widths, x, edge, out, *scratch):
    from_up = scratch[:chunks]
    from_down = scratch[chunks : 2 * chunks]
    wins = scratch[2 * chunks : 2 * chunks + SLOTS]
    (raw, made, prof, gain, pack_up, pack_down, edge_v, len_up, len_down, next_up, next_down, base_up, base_down,
     slot_up, slot_down, in_send, in_recv, in_own, halo_send, halo_recv, far_send, far_recv, out_send,
     out_recv, out_own, edge_sem, off_ref, bw_ref, table_sem) = scratch[2 * chunks + SLOTS :]
    local = x.shape[0]
    rows = x.shape[1] // group
    block = local * group
    hi = after(block)
    own_at = block + LO
    raw_at = LO + SWEEPS
    n_raw = raw.shape[1]
    ext = LO + block + hi
    spans = block // ROWS
    reach = 2 * block + ext
    me = lax.axis_index("scan")
    k = lax.rem(me, group)
    z = lax.div(me, group)
    tile_count = rows // ROWS
    pair = 2 if tile_count % 2 == 0 else 1

    def rows_of(j):
        return pl.ds(pl.multiple_of(j * rows, ROWS), rows)

    def cols_of(c):
        return pl.ds(c * LANES, LANES)

    mates = sorted(range(1, group), key=lambda m: -m.bit_count())

    def partner(m):
        at, bit = k, 1
        while bit < group:
            if m & bit:
                at = at + bit - 2 * bit * lax.rem(lax.div(k, bit), 2)
            bit *= 2
        return at

    def mate(m):
        return z * group + partner(m)

    has = {1: z < LEAD - 1, -1: z > 0}
    gets = {1: z > 0, -1: z < LEAD - 1}

    barrier = pltpu.get_barrier_semaphore()
    for m in mates:
        pl.semaphore_signal(barrier, inc=1, device_id={"scan": mate(m)}, device_id_type=MESH)
    for step in (1, -1):

        @pl.when(has[step])
        def _(step=step):
            pl.semaphore_signal(
                barrier, inc=1, device_id={"scan": me + step * group}, device_id_type=MESH
            )

    count = group - 1
    for step in (1, -1):
        count = count + has[step].astype(jnp.int32)
    pl.semaphore_wait(barrier, count)

    def in_copy(c, m):
        return pltpu.make_async_remote_copy(
            src_ref=x.at[:, rows_of(partner(m)), cols_of(c)],
            dst_ref=raw.at[c, pl.ds(raw_at + k * local, local)],
            send_sem=in_send.at[c, m - 1],
            recv_sem=in_recv.at[c, m - 1],
            device_id={"scan": mate(m)},
            device_id_type=MESH,
        )

    def in_local(c):
        return pltpu.make_async_copy(
            x.at[:, rows_of(k), cols_of(c)],
            raw.at[c, pl.ds(raw_at + k * local, local)],
            in_own.at[c],
        )

    def out_copy(c, m):
        return pltpu.make_async_remote_copy(
            src_ref=made.at[c % SLOTS, pl.ds(partner(m) * local, local)],
            dst_ref=out.at[:, rows_of(k), cols_of(c)],
            send_sem=out_send.at[c, m - 1],
            recv_sem=out_recv.at[c, m - 1],
            device_id={"scan": mate(m)},
            device_id_type=MESH,
        )

    def out_local(c):
        return pltpu.make_async_copy(
            made.at[c % SLOTS, pl.ds(k * local, local)],
            out.at[:, rows_of(k), cols_of(c)],
            out_own.at[c],
        )

    def z_copy(src, dst, sems, c, i, step):
        send, recv = sems
        return pltpu.make_async_remote_copy(
            src_ref=src,
            dst_ref=dst,
            send_sem=send.at[c, i],
            recv_sem=recv.at[c, i],
            device_id={"scan": me + step * group},
            device_id_type=MESH,
        )

    def halo_copies(c):
        sems = (halo_send, halo_recv)
        up = z_copy(
            raw.at[c, pl.ds(block, raw_at)], raw.at[c, pl.ds(0, raw_at)], sems, c, 0, 1
        )
        down = z_copy(
            raw.at[c, pl.ds(raw_at, hi + SWEEPS)],
            raw.at[c, pl.ds(raw_at + block, hi + SWEEPS)], sems, c, 1, -1,
        )
        return ((1, up), (-1, down))

    def far_copies(c):
        sems = (far_send, far_recv)
        up = z_copy(
            pack_up.at[c % SLOTS], from_up[c].at[pl.ds(spans, room)], sems, c, 0, 1
        )
        down = z_copy(
            pack_down.at[c % SLOTS], from_down[c].at[pl.ds(0, room)], sems, c, 1, -1
        )
        return ((1, up), (-1, down))

    def start(copies):
        for step, copy in copies:
            pl.when(has[step])(copy.start)

    def wait_recv(copies):
        for step, copy in copies:
            pl.when(gets[step])(copy.wait_recv)

    def wait_send(copies):
        for step, copy in copies:
            pl.when(has[step])(copy.wait_send)

    edge_copy = pltpu.make_async_copy(edge.at[rows_of(k)], edge_v, edge_sem)
    for c in range(chunks):
        for m in mates:
            in_copy(c, m).start()
        in_local(c).start()
    edge_copy.start()
    table_copies = [
        pltpu.make_async_copy(src, dst, table_sem.at[i])
        for i, (src, dst) in enumerate(((offsets, off_ref), (widths, bw_ref)))
    ]
    for copy in table_copies:
        copy.start()
    for copy in table_copies:
        copy.wait()

    for lens, nexts, bases in ((len_up, next_up, base_up), (len_down, next_down, base_down)):
        lens[rows] = jnp.int32(1)
        nexts[rows] = jnp.int32(rows)

    def measure(r, base):
        up, down = lengths(off_ref[k * rows + r], block)
        len_up[r], len_down[r] = up, down
        base_up[r], base_down[r] = base[0] + up, base[1]
        return base[0] + up, base[1] + down

    lax.fori_loop(0, rows, measure, (jnp.int32(0), jnp.int32(0)))

    def link(i, _):
        r = rows - 1 - i
        for lens, nexts in ((len_up, next_up), (len_down, next_down)):
            nexts[r] = jnp.where(lens[r + 1] > 0, r + 1, nexts[r + 1])
        return 0

    lax.fori_loop(0, rows, link, 0)

    def assign(j, carry):
        result = []
        lists = ((len_up, next_up, slot_up, own_at + block - LO), (len_down, next_down, slot_down, own_at + hi))
        for i, (lens, nexts, slots, first) in enumerate(lists):
            row, p = carry[2 * i], carry[2 * i + 1]
            n = lens[row]
            frame = first + ROWS * p - (ROWS * n if i == 0 else 0)
            slots[j] = jnp.where(row < rows, row * reach + frame, own_at)
            done = p + 1 >= n
            result.append(jnp.where(done, nexts[row], row))
            result.append(jnp.where(done, 0, p + 1))
        return tuple(result)

    heads = []
    for lens, nexts in ((len_up, next_up), (len_down, next_down)):
        heads.append(jnp.where(lens[0] > 0, 0, nexts[0]))
        heads.append(jnp.int32(0))
    lax.fori_loop(0, room, assign, tuple(heads))

    def arrive(c):
        in_local(c).wait()
        for m in mates:
            in_copy(c, m).wait_recv()
        start(halo_copies(c))

    def across(win, tile, frame):
        return win.at[pl.ds(tile * (ROWS * reach) + frame, ROWS, stride=reach)]

    def smooth(c):
        win = wins[c % SLOTS]
        wait_recv(halo_copies(c))

        @pl.when(z == 0)
        def _():
            for i in range(raw_at):
                raw[c, raw_at - 1 - i] = raw[c, raw_at + i]

        @pl.when(z == LEAD - 1)
        def _():
            for i in range(hi + SWEEPS):
                raw[c, raw_at + block + i] = raw[c, raw_at + block - 1 - i]

        def one(p, _):
            def load(t, s):
                at = pl.ds(pl.multiple_of((p * pair + s) * ROWS, ROWS), ROWS)
                return raw[c, t, at, :] * (1.0 / UNIT)

            def store(t, s, value):
                across(win, p * pair + s, block + t)[...] = value

            sweep_pass(load, store, n_raw, ext, SWEEPS, pair)
            return 0

        lax.fori_loop(0, tile_count // pair, one, 0)

        def repeat(first, number, source):
            values = [across(win, p, source)[...] for p in range(tile_count)]

            def one(i, _):
                for p in range(tile_count):
                    across(win, p, first + i)[...] = values[p]
                return 0

            lax.fori_loop(0, number, one, 0)

        pl.when(z == 0)(lambda: repeat(0, own_at, own_at))
        pl.when(z == LEAD - 1)(lambda: repeat(own_at + block, hi + block, own_at + block - 1))
        if c >= SLOTS:
            wait_send(far_copies(c - SLOTS))

        def pack(j, _):
            for slots, packed in ((slot_up, pack_up), (slot_down, pack_down)):
                packed[c % SLOTS, j] = win[pl.ds(slots[j], ROWS), :]
            return 0

        lax.fori_loop(0, room, pack, 0, unroll=4)
        start(far_copies(c))

    def unpack(win, source, bases, first):
        def one(r, _):
            base = bases[r]
            for m in range(spans):
                to = pl.multiple_of(r * reach + first + ROWS * m, ROWS)
                win[pl.ds(to, ROWS), :] = source[base + m]
            return 0

        lax.fori_loop(0, rows, one, 0)

    def depth(c):
        win = wins[c % SLOTS]
        wait_recv(far_copies(c))
        pl.when(gets[1])(lambda: unpack(win, from_up[c], base_up, 0))
        pl.when(gets[-1])(lambda: unpack(win, from_down[c], base_down, own_at + block + hi))

        for p in range(tile_count):
            tile = pl.ds(p * ROWS, ROWS)
            gain[tile, :] = LEVEL_SCALE / edge_v[tile, pl.ds(c * LANES, LANES)].astype(jnp.float32)

        def fill(r, _):
            width = bw_ref[k * rows + r]
            at_b = r * reach + own_at - DIFFUSE + 1 - off_ref[k * rows + r]
            at_a = at_b - width
            scale = jnp.broadcast_to(gain[pl.ds(r, 1), :], (ROWS, LANES)) / width.astype(jnp.float32)
            for m in range(prof.shape[0] // (rows * ROWS)):
                a = win[pl.ds(at_a + m * ROWS, ROWS), :]
                b = win[pl.ds(at_b + m * ROWS, ROWS), :]
                prof[pl.ds(m * ROWS * rows + r, ROWS, stride=rows), :] = (a - b) * scale
            return 0

        lax.fori_loop(0, rows, fill, 0)

        def bins(d):
            return pl.ds(d * rows, rows)

        @pl.when(z == 0)
        def _():
            for i in range(DIFFUSE):
                prof[bins(DIFFUSE - 1 - i), :] = prof[bins(DIFFUSE + i), :]

        @pl.when(z == LEAD - 1)
        def _():
            for i in range(DIFFUSE):
                prof[bins(DIFFUSE + block + i), :] = prof[bins(DIFFUSE + block - 1 - i), :]

        def one(p, _):
            tiles = [pl.ds(pl.multiple_of((p * pair + s) * ROWS, ROWS), ROWS) for s in range(pair)]
            scales = [
                edge_v[tile, pl.ds(c * LANES, LANES)].astype(jnp.float32) * (UNIT / LEVEL_SCALE) for tile in tiles
            ]

            def load(t, s):
                return prof[pl.ds(pl.multiple_of(t * rows + (p * pair + s) * ROWS, ROWS), ROWS), :]

            def store(t, s, value):
                made[c % SLOTS, t, tiles[s], :] = value * scales[s]

            sweep_pass(load, store, block + 2 * DIFFUSE, block, DIFFUSE, pair)
            return 0

        if c >= SLOTS:
            sent(c - SLOTS)
        lax.fori_loop(0, tile_count // pair, one, 0)
        for m in mates:
            out_copy(c, m).start()
        out_local(c).start()

    def sent(c):
        out_local(c).wait()
        for m in mates:
            out_copy(c, m).wait_send()

    arrive(0)
    for c in range(chunks):
        if c + 1 < chunks:
            arrive(c + 1)
        smooth(c)
        if c == 0:
            edge_copy.wait()
        if c >= LAG:
            depth(c - LAG)
    for c in range(max(chunks - LAG, 0), chunks):
        depth(c)
    for c in range(chunks):
        for m in mates:
            in_copy(c, m).wait_send()
        wait_send(halo_copies(c))
        if c >= chunks - SLOTS:
            wait_send(far_copies(c))
        if c >= chunks - SLOTS:
            sent(c)
        for m in mates:
            out_copy(c, m).wait_recv()


def body(frames, depth_offset, band_width, edge_level):
    group = lax.axis_size("scan") // LEAD
    local, all_rows, cols = frames.shape
    chunks, rows, block = cols // LANES, all_rows // group, local * group
    hi, spans = after(block), block // ROWS
    bins = -(-(block + 2 * DIFFUSE) // ROWS) * ROWS
    dma = pltpu.SemaphoreType.DMA
    anywhere = pl.BlockSpec(memory_space=pl.ANY)

    def vmem(*shape):
        return pltpu.VMEM(shape, jnp.float32)

    def table(size):
        return pltpu.SMEM((size,), jnp.int32)

    def with_room(room, call):
        arrived = vmem(spans + room, ROWS, LANES)
        packed = vmem(SLOTS, room, ROWS, LANES)
        return pl.pallas_call(
            functools.partial(kernel, group, chunks, room),
            out_shape=jax.ShapeDtypeStruct(frames.shape, frames.dtype),
            in_specs=[anywhere] * 4,
            out_specs=anywhere,
            scratch_shapes=[arrived] * (2 * chunks)
            + [vmem((3 * block + LO + hi) * rows, LANES)] * SLOTS
            + [
                vmem(chunks, LO + block + hi + 2 * SWEEPS, rows, LANES),
                vmem(SLOTS, block, rows, LANES),
                vmem(bins * rows, LANES),
                vmem(rows, LANES),
                packed,
                packed,
                pltpu.VMEM((rows, cols), jnp.int32),
            ]
            + [table(rows + 1)] * 6
            + [table(room)] * 2
            + [
                dma((chunks, group - 1)),
                dma((chunks, group - 1)),
                dma((chunks,)),
                dma((chunks, 2)),
                dma((chunks, 2)),
                dma((chunks, 2)),
                dma((chunks, 2)),
                dma((chunks, group - 1)),
                dma((chunks, group - 1)),
                dma((chunks,)),
                dma,
                table(all_rows),
                table(all_rows),
                dma((2,)),
            ],
            compiler_params=pltpu.CompilerParams(
                collective_id=call, has_side_effects=True, vmem_limit_bytes=52 * 1024 * 1024
            ),
        )

    whole = rows * spans
    half = whole // 2
    up, down = lengths(depth_offset, block)
    mine = jnp.arange(all_rows)[None] // rows == jnp.arange(group)[:, None]
    taken = jnp.sum(jnp.where(mine, up + down * (2 * whole), 0), 1)
    fits = jnp.max(jnp.maximum(lax.rem(taken, 2 * whole), lax.div(taken, 2 * whole))) <= half
    return lax.cond(
        fits, with_room(half, 0), with_room(whole, 1), depth_offset, band_width, frames, edge_level
    )


def solution(mesh):
    placed = (P("scan", None, "col"), P(), P(), P(None, "col"))
    return jax.shard_map(
        body, mesh=mesh, in_specs=placed, out_specs=P("scan", None, "col"), check_vma=False
    )
```

```python
import functools

import jax
import jax.numpy as jnp
from jax import lax
from jax.experimental import pallas as pl
from jax.experimental.pallas import tpu as pltpu
from jax.sharding import PartitionSpec as P

SWEEPS = 6
DIFFUSE = 6
BAND = 8
STEP_SIZE = 0.24
LEVEL_SCALE = 16.0
LANES = 128
ROWS = 8
LEAD = 4
LAG = 1
SLOTS = 3
UNROLL = 4
LO = DIFFUSE + BAND - 1
MESH = pl.DeviceIdType.MESH
RATE = 1.0 / STEP_SIZE
UNIT = STEP_SIZE**0.5


def after(block):
    least = DIFFUSE + 1
    return least + -(LO + block + least) % ROWS


def lengths(offset, block):
    beyond = -offset + (DIFFUSE + 1 - after(block))
    up = (jnp.maximum(offset, 0) + ROWS - 1) // ROWS
    down = (jnp.maximum(beyond, 0) + ROWS - 1) // ROWS
    return up, down


def sweep_pass(load, store, n_in, n_out, sweeps, streams):
    lead = (n_in - n_out) // 2 + 2 * sweeps - 1

    def advance(t, carry):
        held, flux, made = carry
        at = jnp.minimum(t, n_in - 1)
        new_held, new_flux, new_made = [], [], []
        for s in range(streams):
            fresh = load(at, s)
            for level in range(sweeps):
                k = s * sweeps + level
                b = fresh if level == 0 else made[k - 1]
                a = held[k]
                c = b - a
                d = RATE + c * c
                q = pl.reciprocal(d, approx=True)
                f = c * (q * (2.0 - d * q))
                new_made.append(a + (f - flux[k]))
                new_held.append(b)
                new_flux.append(f)
        return tuple(new_held), tuple(new_flux), tuple(new_made)

    def work(t, carry):
        carry = advance(t + lead, carry)
        for s in range(streams):
            store(t, s, carry[2][s * sweeps + sweeps - 1])
        return carry

    start = tuple(load(0, s) for s in range(streams) for _ in range(sweeps))
    carry = lax.fori_loop(0, lead, advance, (start, start, start))
    lax.fori_loop(0, n_out, work, carry, unroll=UNROLL)


def kernel(group, chunks, room, offsets, widths, x, edge, out, *scratch):
    from_up = scratch[:chunks]
    from_down = scratch[chunks : 2 * chunks]
    wins = scratch[2 * chunks : 2 * chunks + SLOTS]
    (raw, made, prof, gain, pack_up, pack_down, edge_v, len_up, len_down, next_up, next_down, base_up, base_down,
     slot_up, slot_down, in_send, in_recv, in_own, halo_send, halo_recv, far_send, far_recv, out_send,
     out_recv, out_own, edge_sem, off_ref, bw_ref, table_sem) = scratch[2 * chunks + SLOTS :]
    local = x.shape[0]
    rows = x.shape[1] // group
    block = local * group
    hi = after(block)
    own_at = block + LO
    raw_at = LO + SWEEPS
    n_raw = raw.shape[1]
    ext = LO + block + hi
    spans = block // ROWS
    reach = 2 * block + ext
    me = lax.axis_index("scan")
    k = lax.rem(me, group)
    z = lax.div(me, group)
    tile_count = rows // ROWS
    pair = 2 if tile_count % 2 == 0 else 1

    def rows_of(j):
        return pl.ds(pl.multiple_of(j * rows, ROWS), rows)

    def cols_of(c):
        return pl.ds(c * LANES, LANES)

    mates = sorted(range(1, group), key=lambda m: -m.bit_count())

    def partner(m):
        at, bit = k, 1
        while bit < group:
            if m & bit:
                at = at + bit - 2 * bit * lax.rem(lax.div(k, bit), 2)
            bit *= 2
        return at

    def mate(m):
        return z * group + partner(m)

    has = {1: z < LEAD - 1, -1: z > 0}
    gets = {1: z > 0, -1: z < LEAD - 1}

    barrier = pltpu.get_barrier_semaphore()
    for m in mates:
        pl.semaphore_signal(barrier, inc=1, device_id={"scan": mate(m)}, device_id_type=MESH)
    for step in (1, -1):

        @pl.when(has[step])
        def _(step=step):
            pl.semaphore_signal(
                barrier, inc=1, device_id={"scan": me + step * group}, device_id_type=MESH
            )

    count = group - 1
    for step in (1, -1):
        count = count + has[step].astype(jnp.int32)
    pl.semaphore_wait(barrier, count)

    def in_copy(c, m):
        return pltpu.make_async_remote_copy(
            src_ref=x.at[:, rows_of(partner(m)), cols_of(c)],
            dst_ref=raw.at[c, pl.ds(raw_at + k * local, local)],
            send_sem=in_send.at[c, m - 1],
            recv_sem=in_recv.at[c, m - 1],
            device_id={"scan": mate(m)},
            device_id_type=MESH,
        )

    def in_local(c):
        return pltpu.make_async_copy(
            x.at[:, rows_of(k), cols_of(c)],
            raw.at[c, pl.ds(raw_at + k * local, local)],
            in_own.at[c],
        )

    def out_copy(c, m):
        return pltpu.make_async_remote_copy(
            src_ref=made.at[c % SLOTS, pl.ds(partner(m) * local, local)],
            dst_ref=out.at[:, rows_of(k), cols_of(c)],
            send_sem=out_send.at[c, m - 1],
            recv_sem=out_recv.at[c, m - 1],
            device_id={"scan": mate(m)},
            device_id_type=MESH,
        )

    def out_local(c):
        return pltpu.make_async_copy(
            made.at[c % SLOTS, pl.ds(k * local, local)],
            out.at[:, rows_of(k), cols_of(c)],
            out_own.at[c],
        )

    def z_copy(src, dst, sems, c, i, step):
        send, recv = sems
        return pltpu.make_async_remote_copy(
            src_ref=src,
            dst_ref=dst,
            send_sem=send.at[c, i],
            recv_sem=recv.at[c, i],
            device_id={"scan": me + step * group},
            device_id_type=MESH,
        )

    def halo_copies(c):
        sems = (halo_send, halo_recv)
        up = z_copy(
            raw.at[c, pl.ds(block, raw_at)], raw.at[c, pl.ds(0, raw_at)], sems, c, 0, 1
        )
        down = z_copy(
            raw.at[c, pl.ds(raw_at, hi + SWEEPS)],
            raw.at[c, pl.ds(raw_at + block, hi + SWEEPS)], sems, c, 1, -1,
        )
        return ((1, up), (-1, down))

    def far_copies(c):
        sems = (far_send, far_recv)
        up = z_copy(
            pack_up.at[c % SLOTS], from_up[c].at[pl.ds(spans, room)], sems, c, 0, 1
        )
        down = z_copy(
            pack_down.at[c % SLOTS], from_down[c].at[pl.ds(0, room)], sems, c, 1, -1
        )
        return ((1, up), (-1, down))

    def start(copies):
        for step, copy in copies:
            pl.when(has[step])(copy.start)

    def wait_recv(copies):
        for step, copy in copies:
            pl.when(gets[step])(copy.wait_recv)

    def wait_send(copies):
        for step, copy in copies:
            pl.when(has[step])(copy.wait_send)

    edge_copy = pltpu.make_async_copy(edge.at[rows_of(k)], edge_v, edge_sem)
    for c in range(chunks):
        for m in mates:
            in_copy(c, m).start()
        in_local(c).start()
    edge_copy.start()
    table_copies = [
        pltpu.make_async_copy(src, dst, table_sem.at[i])
        for i, (src, dst) in enumerate(((offsets, off_ref), (widths, bw_ref)))
    ]
    for copy in table_copies:
        copy.start()
    for copy in table_copies:
        copy.wait()

    for lens, nexts, bases in ((len_up, next_up, base_up), (len_down, next_down, base_down)):
        lens[rows] = jnp.int32(1)
        nexts[rows] = jnp.int32(rows)

    def measure(r, base):
        up, down = lengths(off_ref[k * rows + r], block)
        len_up[r], len_down[r] = up, down
        base_up[r], base_down[r] = base[0] + up, base[1]
        return base[0] + up, base[1] + down

    lax.fori_loop(0, rows, measure, (jnp.int32(0), jnp.int32(0)))

    def link(i, _):
        r = rows - 1 - i
        for lens, nexts in ((len_up, next_up), (len_down, next_down)):
            nexts[r] = jnp.where(lens[r + 1] > 0, r + 1, nexts[r + 1])
        return 0

    lax.fori_loop(0, rows, link, 0)

    def assign(j, carry):
        result = []
        lists = ((len_up, next_up, slot_up, own_at + block - LO), (len_down, next_down, slot_down, own_at + hi))
        for i, (lens, nexts, slots, first) in enumerate(lists):
            row, p = carry[2 * i], carry[2 * i + 1]
            n = lens[row]
            frame = first + ROWS * p - (ROWS * n if i == 0 else 0)
            slots[j] = jnp.where(row < rows, row * reach + frame, own_at)
            done = p + 1 >= n
            result.append(jnp.where(done, nexts[row], row))
            result.append(jnp.where(done, 0, p + 1))
        return tuple(result)

    heads = []
    for lens, nexts in ((len_up, next_up), (len_down, next_down)):
        heads.append(jnp.where(lens[0] > 0, 0, nexts[0]))
        heads.append(jnp.int32(0))
    lax.fori_loop(0, room, assign, tuple(heads))

    def arrive(c):
        in_local(c).wait()
        for m in mates:
            in_copy(c, m).wait_recv()
        start(halo_copies(c))

    def across(win, tile, frame):
        return win.at[pl.ds(tile * (ROWS * reach) + frame, ROWS, stride=reach)]

    def smooth(c):
        win = wins[c % SLOTS]
        wait_recv(halo_copies(c))

        @pl.when(z == 0)
        def _():
            for i in range(raw_at):
                raw[c, raw_at - 1 - i] = raw[c, raw_at + i]

        @pl.when(z == LEAD - 1)
        def _():
            for i in range(hi + SWEEPS):
                raw[c, raw_at + block + i] = raw[c, raw_at + block - 1 - i]

        def one(p, _):
            def load(t, s):
                at = pl.ds(pl.multiple_of((p * pair + s) * ROWS, ROWS), ROWS)
                return raw[c, t, at, :] * (1.0 / UNIT)

            def store(t, s, value):
                across(win, p * pair + s, block + t)[...] = value

            sweep_pass(load, store, n_raw, ext, SWEEPS, pair)
            return 0

        lax.fori_loop(0, tile_count // pair, one, 0)

        def repeat(first, number, source):
            values = [across(win, p, source)[...] for p in range(tile_count)]

            def one(i, _):
                for p in range(tile_count):
                    across(win, p, first + i)[...] = values[p]
                return 0

            lax.fori_loop(0, number, one, 0)

        pl.when(z == 0)(lambda: repeat(0, own_at, own_at))
        pl.when(z == LEAD - 1)(lambda: repeat(own_at + block, hi + block, own_at + block - 1))
        if c >= SLOTS:
            wait_send(far_copies(c - SLOTS))

        def pack(j, _):
            for slots, packed in ((slot_up, pack_up), (slot_down, pack_down)):
                packed[c % SLOTS, j] = win[pl.ds(slots[j], ROWS), :]
            return 0

        lax.fori_loop(0, room, pack, 0, unroll=4)
        start(far_copies(c))

    def unpack(win, source, bases, first):
        def one(r, _):
            base = bases[r]
            for m in range(spans):
                to = pl.multiple_of(r * reach + first + ROWS * m, ROWS)
                win[pl.ds(to, ROWS), :] = source[base + m]
            return 0

        lax.fori_loop(0, rows, one, 0)

    def depth(c):
        win = wins[c % SLOTS]
        wait_recv(far_copies(c))
        pl.when(gets[1])(lambda: unpack(win, from_up[c], base_up, 0))
        pl.when(gets[-1])(lambda: unpack(win, from_down[c], base_down, own_at + block + hi))

        for p in range(tile_count):
            tile = pl.ds(p * ROWS, ROWS)
            gain[tile, :] = LEVEL_SCALE / edge_v[tile, pl.ds(c * LANES, LANES)].astype(jnp.float32)

        def fill(r, _):
            width = bw_ref[k * rows + r]
            at_b = r * reach + own_at - DIFFUSE + 1 - off_ref[k * rows + r]
            at_a = at_b - width
            scale = jnp.broadcast_to(gain[pl.ds(r, 1), :], (ROWS, LANES)) / width.astype(jnp.float32)
            for m in range(prof.shape[0] // (rows * ROWS)):
                a = win[pl.ds(at_a + m * ROWS, ROWS), :]
                b = win[pl.ds(at_b + m * ROWS, ROWS), :]
                prof[pl.ds(m * ROWS * rows + r, ROWS, stride=rows), :] = (a - b) * scale
            return 0

        lax.fori_loop(0, rows, fill, 0)

        def bins(d):
            return pl.ds(d * rows, rows)

        @pl.when(z == 0)
        def _():
            for i in range(DIFFUSE):
                prof[bins(DIFFUSE - 1 - i), :] = prof[bins(DIFFUSE + i), :]

        @pl.when(z == LEAD - 1)
        def _():
            for i in range(DIFFUSE):
                prof[bins(DIFFUSE + block + i), :] = prof[bins(DIFFUSE + block - 1 - i), :]

        def one(p, _):
            tiles = [pl.ds(pl.multiple_of((p * pair + s) * ROWS, ROWS), ROWS) for s in range(pair)]
            scales = [
                edge_v[tile, pl.ds(c * LANES, LANES)].astype(jnp.float32) * (UNIT / LEVEL_SCALE) for tile in tiles
            ]

            def load(t, s):
                return prof[pl.ds(pl.multiple_of(t * rows + (p * pair + s) * ROWS, ROWS), ROWS), :]

            def store(t, s, value):
                made[c % SLOTS, t, tiles[s], :] = value * scales[s]

            sweep_pass(load, store, block + 2 * DIFFUSE, block, DIFFUSE, pair)
            return 0

        if c >= SLOTS:
            sent(c - SLOTS)
        lax.fori_loop(0, tile_count // pair, one, 0)
        for m in mates:
            out_copy(c, m).start()
        out_local(c).start()

    def sent(c):
        out_local(c).wait()
        for m in mates:
            out_copy(c, m).wait_send()

    arrive(0)
    for c in range(chunks):
        if c + 1 < chunks:
            arrive(c + 1)
        smooth(c)
        if c == 0:
            edge_copy.wait()
        if c >= LAG:
            depth(c - LAG)
    for c in range(max(chunks - LAG, 0), chunks):
        depth(c)
    for c in range(chunks):
        for m in mates:
            in_copy(c, m).wait_send()
        wait_send(halo_copies(c))
        if c >= chunks - SLOTS:
            wait_send(far_copies(c))
        if c >= chunks - SLOTS:
            sent(c)
        for m in mates:
            out_copy(c, m).wait_recv()


def decide(group, block, room, offsets, over):
    shape = (group, offsets.shape[1])
    rows = shape[1] // group
    slot = lax.broadcasted_iota(jnp.int32, shape, 1) - rows * lax.broadcasted_iota(jnp.int32, shape, 0)
    most = 0.0
    for n in lengths(offsets[...], block):
        n = jnp.broadcast_to(n.astype(jnp.float32), shape)
        most = jnp.maximum(most, jnp.sum(jnp.where((slot >= 0) & (slot < rows), n, 0.0), 1, keepdims=True))
    over[0] = (jnp.max(most) > room).astype(jnp.int32)


def choose(index, branches, *operands):
    traced = jax.make_jaxpr(lambda i, *args: lax.switch(i, branches, *args))(index, *operands)
    (switch,) = [eqn for eqn in traced.eqns if eqn.primitive.name == "cond"]
    assert list(switch.invars[1:]) == list(traced.jaxpr.invars[1:]) and not traced.consts
    return switch.primitive.bind(index, *operands, **switch.params)[0]


def body(frames, depth_offset, band_width, edge_level):
    group = lax.axis_size("scan") // LEAD
    local, all_rows, cols = frames.shape
    chunks, rows, block = cols // LANES, all_rows // group, local * group
    hi, spans = after(block), block // ROWS
    bins = -(-(block + 2 * DIFFUSE) // ROWS) * ROWS
    dma = pltpu.SemaphoreType.DMA
    anywhere = pl.BlockSpec(memory_space=pl.ANY)

    def vmem(*shape):
        return pltpu.VMEM(shape, jnp.float32)

    def table(size):
        return pltpu.SMEM((size,), jnp.int32)

    def with_room(room, call):
        arrived = vmem(spans + room, ROWS, LANES)
        packed = vmem(SLOTS, room, ROWS, LANES)
        return pl.pallas_call(
            functools.partial(kernel, group, chunks, room),
            out_shape=jax.ShapeDtypeStruct(frames.shape, frames.dtype),
            in_specs=[anywhere] * 4,
            out_specs=anywhere,
            scratch_shapes=[arrived] * (2 * chunks)
            + [vmem((3 * block + LO + hi) * rows, LANES)] * SLOTS
            + [
                vmem(chunks, LO + block + hi + 2 * SWEEPS, rows, LANES),
                vmem(SLOTS, block, rows, LANES),
                vmem(bins * rows, LANES),
                vmem(rows, LANES),
                packed,
                packed,
                pltpu.VMEM((rows, cols), jnp.int32),
            ]
            + [table(rows + 1)] * 6
            + [table(room)] * 2
            + [
                dma((chunks, group - 1)),
                dma((chunks, group - 1)),
                dma((chunks,)),
                dma((chunks, 2)),
                dma((chunks, 2)),
                dma((chunks, 2)),
                dma((chunks, 2)),
                dma((chunks, group - 1)),
                dma((chunks, group - 1)),
                dma((chunks,)),
                dma,
                table(all_rows),
                table(all_rows),
                dma((2,)),
            ],
            compiler_params=pltpu.CompilerParams(
                collective_id=call, has_side_effects=True, vmem_limit_bytes=52 * 1024 * 1024
            ),
        )

    whole = rows * spans
    half = whole // 2
    over = pl.pallas_call(
        functools.partial(decide, group, block, half),
        out_shape=pltpu.SMEM((1,), jnp.int32),
        in_specs=[pl.BlockSpec(memory_space=pltpu.VMEM)],
        out_specs=pl.BlockSpec(memory_space=pltpu.SMEM),
    )(depth_offset[None])
    kernels = [with_room(half, 0), with_room(whole, 1)]
    return choose(over.reshape(()), kernels, depth_offset, band_width, frames, edge_level)


def solution(mesh):
    placed = (P("scan", None, "col"), P(), P(), P(None, "col"))
    return jax.shard_map(
        body, mesh=mesh, in_specs=placed, out_specs=P("scan", None, "col"), check_vma=False
    )
```

```python
import functools

import jax
import jax.numpy as jnp
from jax import lax
from jax.experimental import pallas as pl
from jax.experimental.pallas import tpu as pltpu
from jax.sharding import PartitionSpec as P

SWEEPS = 6
DIFFUSE = 6
BAND = 8
STEP_SIZE = 0.24
LEVEL_SCALE = 16.0
LANES = 128
ROWS = 8
LEAD = 4
LAG = 1
SLOTS = 3
BUFFERS = 2
UNROLL = 4
LO = DIFFUSE + BAND - 1
MESH = pl.DeviceIdType.MESH
RATE = 1.0 / STEP_SIZE
UNIT = STEP_SIZE**0.5


def after(block):
    least = DIFFUSE + 1
    return least + -(LO + block + least) % ROWS


def lengths(offset, block):
    beyond = -offset + (DIFFUSE + 1 - after(block))
    up = (jnp.maximum(offset, 0) + ROWS - 1) // ROWS
    down = (jnp.maximum(beyond, 0) + ROWS - 1) // ROWS
    return up, down


def out_parts(chunks):
    parts, c = [], 0
    while c < chunks:
        wide = 2 if c + 2 <= chunks - 2 else 1
        parts.append((c, wide))
        c += wide
    return parts


def sweep_pass(load, store, n_in, n_out, sweeps, streams):
    lead = (n_in - n_out) // 2 + 2 * sweeps - 1

    def advance(t, carry):
        held, flux, made = carry
        at = jnp.minimum(t, n_in - 1)
        new_held, new_flux, new_made = [], [], []
        for s in range(streams):
            fresh = load(at, s)
            for level in range(sweeps):
                k = s * sweeps + level
                b = fresh if level == 0 else made[k - 1]
                a = held[k]
                c = b - a
                d = RATE + c * c
                q = pl.reciprocal(d, approx=True)
                f = c * (q * (2.0 - d * q))
                new_made.append(a + (f - flux[k]))
                new_held.append(b)
                new_flux.append(f)
        return tuple(new_held), tuple(new_flux), tuple(new_made)

    def work(t, carry):
        carry = advance(t + lead, carry)
        for s in range(streams):
            store(t, s, carry[2][s * sweeps + sweeps - 1])
        return carry

    start = tuple(load(0, s) for s in range(streams) for _ in range(sweeps))
    carry = lax.fori_loop(0, lead, advance, (start, start, start))
    lax.fori_loop(0, n_out, work, carry, unroll=UNROLL)


def kernel(group, chunks, room, offsets, widths, x, edge, out, *scratch):
    from_up = scratch[:chunks]
    from_down = scratch[chunks : 2 * chunks]
    wins = scratch[2 * chunks : 2 * chunks + SLOTS]
    (raw, made, prof, gain, pack_up, pack_down, edge_v, len_up, len_down, next_up, next_down, base_up, base_down,
     slot_up, slot_down, in_send, in_recv, in_own, halo_send, halo_recv, far_send, far_recv, out_send,
     out_recv, out_own, edge_sem, off_ref, bw_ref, table_sem) = scratch[2 * chunks + SLOTS :]
    local = x.shape[0]
    rows = x.shape[1] // group
    block = local * group
    hi = after(block)
    own_at = block + LO
    raw_at = LO + SWEEPS
    n_raw = raw.shape[1]
    ext = LO + block + hi
    spans = block // ROWS
    reach = 2 * block + ext
    me = lax.axis_index("scan")
    k = lax.rem(me, group)
    z = lax.div(me, group)
    tile_count = rows // ROWS
    pair = 2 if tile_count % 2 == 0 else 1
    outs = out_parts(chunks)
    buffer_of = [u for u, part in enumerate(outs) for _ in range(part[1])]

    def rows_of(j):
        return pl.ds(pl.multiple_of(j * rows, ROWS), rows)

    def cols_of(c, wide=1):
        return pl.ds(c * LANES, wide * LANES)

    mates = sorted(range(1, group), key=lambda m: -m.bit_count())

    def partner(m):
        at, bit = k, 1
        while bit < group:
            if m & bit:
                at = at + bit - 2 * bit * lax.rem(lax.div(k, bit), 2)
            bit *= 2
        return at

    def mate(m):
        return z * group + partner(m)

    has = {1: z < LEAD - 1, -1: z > 0}
    gets = {1: z > 0, -1: z < LEAD - 1}

    barrier = pltpu.get_barrier_semaphore()
    for m in mates:
        pl.semaphore_signal(barrier, inc=1, device_id={"scan": mate(m)}, device_id_type=MESH)
    for step in (1, -1):

        @pl.when(has[step])
        def _(step=step):
            pl.semaphore_signal(
                barrier, inc=1, device_id={"scan": me + step * group}, device_id_type=MESH
            )

    count = group - 1
    for step in (1, -1):
        count = count + has[step].astype(jnp.int32)
    pl.semaphore_wait(barrier, count)

    def in_copy(c, m):
        return pltpu.make_async_remote_copy(
            src_ref=x.at[:, rows_of(partner(m)), cols_of(c)],
            dst_ref=raw.at[c, pl.ds(raw_at + k * local, local)],
            send_sem=in_send.at[c, m - 1],
            recv_sem=in_recv.at[c, m - 1],
            device_id={"scan": mate(m)},
            device_id_type=MESH,
        )

    def in_local(c):
        return pltpu.make_async_copy(
            x.at[:, rows_of(k), cols_of(c)],
            raw.at[c, pl.ds(raw_at + k * local, local)],
            in_own.at[c],
        )

    def out_source(u, j):
        c, wide = outs[u]
        return made.at[u % BUFFERS, pl.ds(j * local, local), :, pl.ds(0, wide * LANES)]

    def out_place(u):
        c, wide = outs[u]
        return out.at[:, rows_of(k), cols_of(c, wide)]

    def out_copy(u, m):
        return pltpu.make_async_remote_copy(
            src_ref=out_source(u, partner(m)),
            dst_ref=out_place(u),
            send_sem=out_send.at[u, m - 1],
            recv_sem=out_recv.at[u, m - 1],
            device_id={"scan": mate(m)},
            device_id_type=MESH,
        )

    def out_local(u):
        return pltpu.make_async_copy(out_source(u, k), out_place(u), out_own.at[u])

    def z_copy(src, dst, sems, c, i, step):
        send, recv = sems
        return pltpu.make_async_remote_copy(
            src_ref=src,
            dst_ref=dst,
            send_sem=send.at[c, i],
            recv_sem=recv.at[c, i],
            device_id={"scan": me + step * group},
            device_id_type=MESH,
        )

    def halo_copies(c):
        sems = (halo_send, halo_recv)
        up = z_copy(
            raw.at[c, pl.ds(block, raw_at)], raw.at[c, pl.ds(0, raw_at)], sems, c, 0, 1
        )
        down = z_copy(
            raw.at[c, pl.ds(raw_at, hi + SWEEPS)],
            raw.at[c, pl.ds(raw_at + block, hi + SWEEPS)], sems, c, 1, -1,
        )
        return ((1, up), (-1, down))

    def far_copies(c):
        sems = (far_send, far_recv)
        up = z_copy(
            pack_up.at[c % SLOTS], from_up[c].at[pl.ds(spans, room)], sems, c, 0, 1
        )
        down = z_copy(
            pack_down.at[c % SLOTS], from_down[c].at[pl.ds(0, room)], sems, c, 1, -1
        )
        return ((1, up), (-1, down))

    def start(copies):
        for step, copy in copies:
            pl.when(has[step])(copy.start)

    def wait_recv(copies):
        for step, copy in copies:
            pl.when(gets[step])(copy.wait_recv)

    def wait_send(copies):
        for step, copy in copies:
            pl.when(has[step])(copy.wait_send)

    edge_copy = pltpu.make_async_copy(edge.at[rows_of(k)], edge_v, edge_sem)
    for c in range(chunks):
        for m in mates:
            in_copy(c, m).start()
        in_local(c).start()
    edge_copy.start()
    table_copies = [
        pltpu.make_async_copy(src, dst, table_sem.at[i])
        for i, (src, dst) in enumerate(((offsets, off_ref), (widths, bw_ref)))
    ]
    for copy in table_copies:
        copy.start()
    for copy in table_copies:
        copy.wait()

    for lens, nexts, bases in ((len_up, next_up, base_up), (len_down, next_down, base_down)):
        lens[rows] = jnp.int32(1)
        nexts[rows] = jnp.int32(rows)

    def measure(r, base):
        up, down = lengths(off_ref[k * rows + r], block)
        len_up[r], len_down[r] = up, down
        base_up[r], base_down[r] = base[0] + up, base[1]
        return base[0] + up, base[1] + down

    lax.fori_loop(0, rows, measure, (jnp.int32(0), jnp.int32(0)))

    def link(i, _):
        r = rows - 1 - i
        for lens, nexts in ((len_up, next_up), (len_down, next_down)):
            nexts[r] = jnp.where(lens[r + 1] > 0, r + 1, nexts[r + 1])
        return 0

    lax.fori_loop(0, rows, link, 0)

    def assign(j, carry):
        result = []
        lists = ((len_up, next_up, slot_up, own_at + block - LO), (len_down, next_down, slot_down, own_at + hi))
        for i, (lens, nexts, slots, first) in enumerate(lists):
            row, p = carry[2 * i], carry[2 * i + 1]
            n = lens[row]
            frame = first + ROWS * p - (ROWS * n if i == 0 else 0)
            slots[j] = jnp.where(row < rows, row * reach + frame, own_at)
            done = p + 1 >= n
            result.append(jnp.where(done, nexts[row], row))
            result.append(jnp.where(done, 0, p + 1))
        return tuple(result)

    heads = []
    for lens, nexts in ((len_up, next_up), (len_down, next_down)):
        heads.append(jnp.where(lens[0] > 0, 0, nexts[0]))
        heads.append(jnp.int32(0))
    lax.fori_loop(0, room, assign, tuple(heads))

    def arrive(c):
        in_local(c).wait()
        for m in mates:
            in_copy(c, m).wait_recv()
        start(halo_copies(c))

    def across(win, tile, frame):
        return win.at[pl.ds(tile * (ROWS * reach) + frame, ROWS, stride=reach)]

    def smooth(c):
        win = wins[c % SLOTS]
        wait_recv(halo_copies(c))

        @pl.when(z == 0)
        def _():
            for i in range(raw_at):
                raw[c, raw_at - 1 - i] = raw[c, raw_at + i]

        @pl.when(z == LEAD - 1)
        def _():
            for i in range(hi + SWEEPS):
                raw[c, raw_at + block + i] = raw[c, raw_at + block - 1 - i]

        def one(p, _):
            def load(t, s):
                at = pl.ds(pl.multiple_of((p * pair + s) * ROWS, ROWS), ROWS)
                return raw[c, t, at, :] * (1.0 / UNIT)

            def store(t, s, value):
                across(win, p * pair + s, block + t)[...] = value

            sweep_pass(load, store, n_raw, ext, SWEEPS, pair)
            return 0

        lax.fori_loop(0, tile_count // pair, one, 0)

        def repeat(first, number, source):
            values = [across(win, p, source)[...] for p in range(tile_count)]

            def one(i, _):
                for p in range(tile_count):
                    across(win, p, first + i)[...] = values[p]
                return 0

            lax.fori_loop(0, number, one, 0)

        pl.when(z == 0)(lambda: repeat(0, own_at, own_at))
        pl.when(z == LEAD - 1)(lambda: repeat(own_at + block, hi + block, own_at + block - 1))
        if c >= SLOTS:
            wait_send(far_copies(c - SLOTS))

        def pack(j, _):
            for slots, packed in ((slot_up, pack_up), (slot_down, pack_down)):
                packed[c % SLOTS, j] = win[pl.ds(slots[j], ROWS), :]
            return 0

        lax.fori_loop(0, room, pack, 0, unroll=4)
        start(far_copies(c))

    def unpack(win, source, bases, first):
        def one(r, _):
            base = bases[r]
            for m in range(spans):
                to = pl.multiple_of(r * reach + first + ROWS * m, ROWS)
                win[pl.ds(to, ROWS), :] = source[base + m]
            return 0

        lax.fori_loop(0, rows, one, 0)

    def depth(c):
        u = buffer_of[c]
        win = wins[c % SLOTS]
        wait_recv(far_copies(c))
        pl.when(gets[1])(lambda: unpack(win, from_up[c], base_up, 0))
        pl.when(gets[-1])(lambda: unpack(win, from_down[c], base_down, own_at + block + hi))

        for p in range(tile_count):
            tile = pl.ds(p * ROWS, ROWS)
            gain[tile, :] = LEVEL_SCALE / edge_v[tile, pl.ds(c * LANES, LANES)].astype(jnp.float32)

        def fill(r, _):
            width = bw_ref[k * rows + r]
            at_b = r * reach + own_at - DIFFUSE + 1 - off_ref[k * rows + r]
            at_a = at_b - width
            scale = jnp.broadcast_to(gain[pl.ds(r, 1), :], (ROWS, LANES)) / width.astype(jnp.float32)
            for m in range(prof.shape[0] // (rows * ROWS)):
                a = win[pl.ds(at_a + m * ROWS, ROWS), :]
                b = win[pl.ds(at_b + m * ROWS, ROWS), :]
                prof[pl.ds(m * ROWS * rows + r, ROWS, stride=rows), :] = (a - b) * scale
            return 0

        lax.fori_loop(0, rows, fill, 0)

        def bins(d):
            return pl.ds(d * rows, rows)

        @pl.when(z == 0)
        def _():
            for i in range(DIFFUSE):
                prof[bins(DIFFUSE - 1 - i), :] = prof[bins(DIFFUSE + i), :]

        @pl.when(z == LEAD - 1)
        def _():
            for i in range(DIFFUSE):
                prof[bins(DIFFUSE + block + i), :] = prof[bins(DIFFUSE + block - 1 - i), :]

        def one(p, _):
            tiles = [pl.ds(pl.multiple_of((p * pair + s) * ROWS, ROWS), ROWS) for s in range(pair)]
            scales = [
                edge_v[tile, pl.ds(c * LANES, LANES)].astype(jnp.float32) * (UNIT / LEVEL_SCALE) for tile in tiles
            ]

            def load(t, s):
                return prof[pl.ds(pl.multiple_of(t * rows + (p * pair + s) * ROWS, ROWS), ROWS), :]

            def store(t, s, value):
                made[u % BUFFERS, t, tiles[s], pl.ds((c - outs[u][0]) * LANES, LANES)] = value * scales[s]

            sweep_pass(load, store, block + 2 * DIFFUSE, block, DIFFUSE, pair)
            return 0

        if c == outs[u][0] and u >= BUFFERS:
            sent(u - BUFFERS)
        lax.fori_loop(0, tile_count // pair, one, 0)
        if c + 1 == sum(outs[u]):
            for m in mates:
                out_copy(u, m).start()
            out_local(u).start()

    def sent(u):
        out_local(u).wait()
        for m in mates:
            out_copy(u, m).wait_send()

    arrive(0)
    for c in range(chunks):
        if c + 1 < chunks:
            arrive(c + 1)
        smooth(c)
        if c == 0:
            edge_copy.wait()
        if c >= LAG:
            depth(c - LAG)
    for c in range(max(chunks - LAG, 0), chunks):
        depth(c)
    for c in range(chunks):
        for m in mates:
            in_copy(c, m).wait_send()
        wait_send(halo_copies(c))
        if c >= chunks - SLOTS:
            wait_send(far_copies(c))
    for u in range(len(outs)):
        if u >= len(outs) - BUFFERS:
            sent(u)
        for m in mates:
            out_copy(u, m).wait_recv()


def decide(group, block, room, offsets, over):
    shape = (group, offsets.shape[1])
    rows = shape[1] // group
    slot = lax.broadcasted_iota(jnp.int32, shape, 1) - rows * lax.broadcasted_iota(jnp.int32, shape, 0)
    most = 0.0
    for n in lengths(offsets[...], block):
        n = jnp.broadcast_to(n.astype(jnp.float32), shape)
        most = jnp.maximum(most, jnp.sum(jnp.where((slot >= 0) & (slot < rows), n, 0.0), 1, keepdims=True))
    over[0] = (jnp.max(most) > room).astype(jnp.int32)


def choose(index, branches, *operands):
    traced = jax.make_jaxpr(lambda i, *args: lax.switch(i, branches, *args))(index, *operands)
    (switch,) = [eqn for eqn in traced.eqns if eqn.primitive.name == "cond"]
    assert list(switch.invars[1:]) == list(traced.jaxpr.invars[1:]) and not traced.consts
    return switch.primitive.bind(index, *operands, **switch.params)[0]


def body(frames, depth_offset, band_width, edge_level):
    group = lax.axis_size("scan") // LEAD
    local, all_rows, cols = frames.shape
    chunks, rows, block = cols // LANES, all_rows // group, local * group
    hi, spans = after(block), block // ROWS
    bins = -(-(block + 2 * DIFFUSE) // ROWS) * ROWS
    n_out = len(out_parts(chunks))
    dma = pltpu.SemaphoreType.DMA
    anywhere = pl.BlockSpec(memory_space=pl.ANY)

    def vmem(*shape):
        return pltpu.VMEM(shape, jnp.float32)

    def table(size):
        return pltpu.SMEM((size,), jnp.int32)

    def with_room(room, call):
        arrived = vmem(spans + room, ROWS, LANES)
        packed = vmem(SLOTS, room, ROWS, LANES)
        return pl.pallas_call(
            functools.partial(kernel, group, chunks, room),
            out_shape=jax.ShapeDtypeStruct(frames.shape, frames.dtype),
            in_specs=[anywhere] * 4,
            out_specs=anywhere,
            scratch_shapes=[arrived] * (2 * chunks)
            + [vmem((3 * block + LO + hi) * rows, LANES)] * SLOTS
            + [
                vmem(chunks, LO + block + hi + 2 * SWEEPS, rows, LANES),
                vmem(BUFFERS, block, rows, 2 * LANES),
                vmem(bins * rows, LANES),
                vmem(rows, LANES),
                packed,
                packed,
                pltpu.VMEM((rows, cols), jnp.int32),
            ]
            + [table(rows + 1)] * 6
            + [table(room)] * 2
            + [
                dma((chunks, group - 1)),
                dma((chunks, group - 1)),
                dma((chunks,)),
                dma((chunks, 2)),
                dma((chunks, 2)),
                dma((chunks, 2)),
                dma((chunks, 2)),
                dma((n_out, group - 1)),
                dma((n_out, group - 1)),
                dma((n_out,)),
                dma,
                table(all_rows),
                table(all_rows),
                dma((2,)),
            ],
            compiler_params=pltpu.CompilerParams(
                collective_id=call, has_side_effects=True, vmem_limit_bytes=54 * 1024 * 1024
            ),
        )

    whole = rows * spans
    half = whole // 2
    over = pl.pallas_call(
        functools.partial(decide, group, block, half),
        out_shape=pltpu.SMEM((1,), jnp.int32),
        in_specs=[pl.BlockSpec(memory_space=pltpu.VMEM)],
        out_specs=pl.BlockSpec(memory_space=pltpu.SMEM),
    )(depth_offset[None])
    kernels = [with_room(half, 0), with_room(whole, 1)]
    return choose(over.reshape(()), kernels, depth_offset, band_width, frames, edge_level)


def solution(mesh):
    placed = (P("scan", None, "col"), P(), P(), P(None, "col"))
    return jax.shard_map(
        body, mesh=mesh, in_specs=placed, out_specs=P("scan", None, "col"), check_vma=False
    )
```

```python
import functools

import jax
import jax.numpy as jnp
from jax import lax
from jax.experimental import pallas as pl
from jax.experimental.pallas import tpu as pltpu
from jax.sharding import PartitionSpec as P

SWEEPS = 6
DIFFUSE = 6
BAND = 8
STEP_SIZE = 0.24
LEVEL_SCALE = 16.0
LANES = 128
ROWS = 8
LEAD = 4
LAG = 1
SLOTS = 3
BUFFERS = 3
UNROLL = 4
LO = DIFFUSE + BAND - 1
MESH = pl.DeviceIdType.MESH
RATE = 1.0 / STEP_SIZE
UNIT = STEP_SIZE**0.5


def after(block):
    least = DIFFUSE + 1
    return least + -(LO + block + least) % ROWS


def lengths(offset, block):
    beyond = -offset + (DIFFUSE + 1 - after(block))
    up = (jnp.maximum(offset, 0) + ROWS - 1) // ROWS
    down = (jnp.maximum(beyond, 0) + ROWS - 1) // ROWS
    return up, down


def out_parts(chunks):
    parts, c = [], 0
    while c < chunks:
        wide = 2 if c + 2 <= chunks - 2 else 1
        parts.append((c, wide))
        c += wide
    return parts


def sweep_pass(load, store, n_in, n_out, sweeps, streams):
    lead = (n_in - n_out) // 2 + 2 * sweeps - 1

    def advance(t, carry):
        held, flux, made = carry
        at = jnp.minimum(t, n_in - 1)
        new_held, new_flux, new_made = [], [], []
        for s in range(streams):
            fresh = load(at, s)
            for level in range(sweeps):
                k = s * sweeps + level
                b = fresh if level == 0 else made[k - 1]
                a = held[k]
                c = b - a
                d = RATE + c * c
                q = pl.reciprocal(d, approx=True)
                f = c * (q * (2.0 - d * q))
                new_made.append(a + (f - flux[k]))
                new_held.append(b)
                new_flux.append(f)
        return tuple(new_held), tuple(new_flux), tuple(new_made)

    def work(t, carry):
        carry = advance(t + lead, carry)
        for s in range(streams):
            store(t, s, carry[2][s * sweeps + sweeps - 1])
        return carry

    start = tuple(load(0, s) for s in range(streams) for _ in range(sweeps))
    carry = lax.fori_loop(0, lead, advance, (start, start, start))
    lax.fori_loop(0, n_out, work, carry, unroll=UNROLL)


def kernel(group, chunks, room, offsets, widths, x, edge, out, *scratch):
    from_up = scratch[:chunks]
    from_down = scratch[chunks : 2 * chunks]
    wins = scratch[2 * chunks : 2 * chunks + SLOTS]
    (raw, made, prof, gain, pack_up, pack_down, edge_v, len_up, len_down, next_up, next_down, base_up, base_down,
     slot_up, slot_down, in_send, in_recv, in_own, halo_send, halo_recv, far_send, far_recv, out_send,
     out_recv, out_own, edge_sem, off_ref, bw_ref, table_sem) = scratch[2 * chunks + SLOTS :]
    local = x.shape[0]
    rows = x.shape[1] // group
    block = local * group
    hi = after(block)
    own_at = block + LO
    raw_at = LO + SWEEPS
    n_raw = raw.shape[1]
    ext = LO + block + hi
    spans = block // ROWS
    reach = 2 * block + ext
    me = lax.axis_index("scan")
    k = lax.rem(me, group)
    z = lax.div(me, group)
    tile_count = rows // ROWS
    pair = 2 if tile_count % 2 == 0 else 1
    outs = out_parts(chunks)
    buffer_of = [u for u, part in enumerate(outs) for _ in range(part[1])]

    def rows_of(j):
        return pl.ds(pl.multiple_of(j * rows, ROWS), rows)

    def cols_of(c, wide=1):
        return pl.ds(c * LANES, wide * LANES)

    mates = sorted(range(1, group), key=lambda m: -m.bit_count())

    def partner(m):
        at, bit = k, 1
        while bit < group:
            if m & bit:
                at = at + bit - 2 * bit * lax.rem(lax.div(k, bit), 2)
            bit *= 2
        return at

    def mate(m):
        return z * group + partner(m)

    has = {1: z < LEAD - 1, -1: z > 0}
    gets = {1: z > 0, -1: z < LEAD - 1}

    barrier = pltpu.get_barrier_semaphore()
    for m in mates:
        pl.semaphore_signal(barrier, inc=1, device_id={"scan": mate(m)}, device_id_type=MESH)
    for step in (1, -1):

        @pl.when(has[step])
        def _(step=step):
            pl.semaphore_signal(
                barrier, inc=1, device_id={"scan": me + step * group}, device_id_type=MESH
            )

    count = group - 1
    for step in (1, -1):
        count = count + has[step].astype(jnp.int32)
    pl.semaphore_wait(barrier, count)

    def in_copy(c, m):
        return pltpu.make_async_remote_copy(
            src_ref=x.at[:, rows_of(partner(m)), cols_of(c)],
            dst_ref=raw.at[c, pl.ds(raw_at + k * local, local)],
            send_sem=in_send.at[c, m - 1],
            recv_sem=in_recv.at[c, m - 1],
            device_id={"scan": mate(m)},
            device_id_type=MESH,
        )

    def in_local(c):
        return pltpu.make_async_copy(
            x.at[:, rows_of(k), cols_of(c)],
            raw.at[c, pl.ds(raw_at + k * local, local)],
            in_own.at[c],
        )

    def out_source(u, j):
        c, wide = outs[u]
        return made.at[u % BUFFERS, pl.ds(j * local, local), :, pl.ds(0, wide * LANES)]

    def out_place(u):
        c, wide = outs[u]
        return out.at[:, rows_of(k), cols_of(c, wide)]

    def out_copy(u, m):
        return pltpu.make_async_remote_copy(
            src_ref=out_source(u, partner(m)),
            dst_ref=out_place(u),
            send_sem=out_send.at[u, m - 1],
            recv_sem=out_recv.at[u, m - 1],
            device_id={"scan": mate(m)},
            device_id_type=MESH,
        )

    def out_local(u):
        return pltpu.make_async_copy(out_source(u, k), out_place(u), out_own.at[u])

    def z_copy(src, dst, sems, c, i, step):
        send, recv = sems
        return pltpu.make_async_remote_copy(
            src_ref=src,
            dst_ref=dst,
            send_sem=send.at[c, i],
            recv_sem=recv.at[c, i],
            device_id={"scan": me + step * group},
            device_id_type=MESH,
        )

    def halo_copies(c):
        sems = (halo_send, halo_recv)
        up = z_copy(
            raw.at[c, pl.ds(block, raw_at)], raw.at[c, pl.ds(0, raw_at)], sems, c, 0, 1
        )
        down = z_copy(
            raw.at[c, pl.ds(raw_at, hi + SWEEPS)],
            raw.at[c, pl.ds(raw_at + block, hi + SWEEPS)], sems, c, 1, -1,
        )
        return ((1, up), (-1, down))

    def far_copies(c):
        sems = (far_send, far_recv)
        up = z_copy(
            pack_up.at[c % SLOTS], from_up[c].at[pl.ds(spans, room)], sems, c, 0, 1
        )
        down = z_copy(
            pack_down.at[c % SLOTS], from_down[c].at[pl.ds(0, room)], sems, c, 1, -1
        )
        return ((1, up), (-1, down))

    def start(copies):
        for step, copy in copies:
            pl.when(has[step])(copy.start)

    def wait_recv(copies):
        for step, copy in copies:
            pl.when(gets[step])(copy.wait_recv)

    def wait_send(copies):
        for step, copy in copies:
            pl.when(has[step])(copy.wait_send)

    edge_copy = pltpu.make_async_copy(edge.at[rows_of(k)], edge_v, edge_sem)
    for c in range(chunks):
        for m in mates:
            in_copy(c, m).start()
        in_local(c).start()
    edge_copy.start()
    table_copies = [
        pltpu.make_async_copy(src, dst, table_sem.at[i])
        for i, (src, dst) in enumerate(((offsets, off_ref), (widths, bw_ref)))
    ]
    for copy in table_copies:
        copy.start()
    for copy in table_copies:
        copy.wait()

    for lens, nexts, bases in ((len_up, next_up, base_up), (len_down, next_down, base_down)):
        lens[rows] = jnp.int32(1)
        nexts[rows] = jnp.int32(rows)

    def measure(r, base):
        up, down = lengths(off_ref[k * rows + r], block)
        len_up[r], len_down[r] = up, down
        base_up[r], base_down[r] = base[0] + up, base[1]
        return base[0] + up, base[1] + down

    lax.fori_loop(0, rows, measure, (jnp.int32(0), jnp.int32(0)))

    def link(i, _):
        r = rows - 1 - i
        for lens, nexts in ((len_up, next_up), (len_down, next_down)):
            nexts[r] = jnp.where(lens[r + 1] > 0, r + 1, nexts[r + 1])
        return 0

    lax.fori_loop(0, rows, link, 0)

    def assign(j, carry):
        result = []
        lists = ((len_up, next_up, slot_up, own_at + block - LO), (len_down, next_down, slot_down, own_at + hi))
        for i, (lens, nexts, slots, first) in enumerate(lists):
            row, p = carry[2 * i], carry[2 * i + 1]
            n = lens[row]
            frame = first + ROWS * p - (ROWS * n if i == 0 else 0)
            slots[j] = jnp.where(row < rows, row * reach + frame, own_at)
            done = p + 1 >= n
            result.append(jnp.where(done, nexts[row], row))
            result.append(jnp.where(done, 0, p + 1))
        return tuple(result)

    heads = []
    for lens, nexts in ((len_up, next_up), (len_down, next_down)):
        heads.append(jnp.where(lens[0] > 0, 0, nexts[0]))
        heads.append(jnp.int32(0))
    lax.fori_loop(0, room, assign, tuple(heads))

    def arrive(c):
        in_local(c).wait()
        for m in mates:
            in_copy(c, m).wait_recv()
        start(halo_copies(c))

    def across(win, tile, frame):
        return win.at[pl.ds(tile * (ROWS * reach) + frame, ROWS, stride=reach)]

    def smooth(c):
        win = wins[c % SLOTS]
        wait_recv(halo_copies(c))

        @pl.when(z == 0)
        def _():
            for i in range(raw_at):
                raw[c, raw_at - 1 - i] = raw[c, raw_at + i]

        @pl.when(z == LEAD - 1)
        def _():
            for i in range(hi + SWEEPS):
                raw[c, raw_at + block + i] = raw[c, raw_at + block - 1 - i]

        def one(p, _):
            def load(t, s):
                at = pl.ds(pl.multiple_of((p * pair + s) * ROWS, ROWS), ROWS)
                return raw[c, t, at, :] * (1.0 / UNIT)

            def store(t, s, value):
                across(win, p * pair + s, block + t)[...] = value

            sweep_pass(load, store, n_raw, ext, SWEEPS, pair)
            return 0

        lax.fori_loop(0, tile_count // pair, one, 0)

        def repeat(first, number, source):
            values = [across(win, p, source)[...] for p in range(tile_count)]

            def one(i, _):
                for p in range(tile_count):
                    across(win, p, first + i)[...] = values[p]
                return 0

            lax.fori_loop(0, number, one, 0)

        pl.when(z == 0)(lambda: repeat(0, own_at, own_at))
        pl.when(z == LEAD - 1)(lambda: repeat(own_at + block, hi + block, own_at + block - 1))
        if c >= SLOTS:
            wait_send(far_copies(c - SLOTS))

        def pack(j, _):
            for slots, packed in ((slot_up, pack_up), (slot_down, pack_down)):
                packed[c % SLOTS, j] = win[pl.ds(slots[j], ROWS), :]
            return 0

        lax.fori_loop(0, room, pack, 0, unroll=4)
        start(far_copies(c))

    def unpack(win, source, bases, first):
        def one(r, _):
            base = bases[r]
            for m in range(spans):
                to = pl.multiple_of(r * reach + first + ROWS * m, ROWS)
                win[pl.ds(to, ROWS), :] = source[base + m]
            return 0

        lax.fori_loop(0, rows, one, 0)

    def depth(c):
        u = buffer_of[c]
        win = wins[c % SLOTS]
        wait_recv(far_copies(c))
        pl.when(gets[1])(lambda: unpack(win, from_up[c], base_up, 0))
        pl.when(gets[-1])(lambda: unpack(win, from_down[c], base_down, own_at + block + hi))

        for p in range(tile_count):
            tile = pl.ds(p * ROWS, ROWS)
            gain[tile, :] = LEVEL_SCALE / edge_v[tile, pl.ds(c * LANES, LANES)].astype(jnp.float32)

        def fill(r, _):
            width = bw_ref[k * rows + r]
            at_b = r * reach + own_at - DIFFUSE + 1 - off_ref[k * rows + r]
            at_a = at_b - width
            scale = jnp.broadcast_to(gain[pl.ds(r, 1), :], (ROWS, LANES)) / width.astype(jnp.float32)
            for m in range(prof.shape[0] // (rows * ROWS)):
                a = win[pl.ds(at_a + m * ROWS, ROWS), :]
                b = win[pl.ds(at_b + m * ROWS, ROWS), :]
                prof[pl.ds(m * ROWS * rows + r, ROWS, stride=rows), :] = (a - b) * scale
            return 0

        lax.fori_loop(0, rows, fill, 0)

        def bins(d):
            return pl.ds(d * rows, rows)

        @pl.when(z == 0)
        def _():
            for i in range(DIFFUSE):
                prof[bins(DIFFUSE - 1 - i), :] = prof[bins(DIFFUSE + i), :]

        @pl.when(z == LEAD - 1)
        def _():
            for i in range(DIFFUSE):
                prof[bins(DIFFUSE + block + i), :] = prof[bins(DIFFUSE + block - 1 - i), :]

        def one(p, _):
            tiles = [pl.ds(pl.multiple_of((p * pair + s) * ROWS, ROWS), ROWS) for s in range(pair)]
            scales = [
                edge_v[tile, pl.ds(c * LANES, LANES)].astype(jnp.float32) * (UNIT / LEVEL_SCALE) for tile in tiles
            ]

            def load(t, s):
                return prof[pl.ds(pl.multiple_of(t * rows + (p * pair + s) * ROWS, ROWS), ROWS), :]

            def store(t, s, value):
                made[u % BUFFERS, t, tiles[s], pl.ds((c - outs[u][0]) * LANES, LANES)] = value * scales[s]

            sweep_pass(load, store, block + 2 * DIFFUSE, block, DIFFUSE, pair)
            return 0

        if c == outs[u][0] and u >= BUFFERS:
            sent(u - BUFFERS)
        lax.fori_loop(0, tile_count // pair, one, 0)
        if c + 1 == sum(outs[u]):
            for m in mates:
                out_copy(u, m).start()
            out_local(u).start()

    def sent(u):
        out_local(u).wait()
        for m in mates:
            out_copy(u, m).wait_send()

    arrive(0)
    for c in range(chunks):
        if c + 1 < chunks:
            arrive(c + 1)
        smooth(c)
        if c == 0:
            edge_copy.wait()
        if c >= LAG:
            depth(c - LAG)
    for c in range(max(chunks - LAG, 0), chunks):
        depth(c)
    for c in range(chunks):
        for m in mates:
            in_copy(c, m).wait_send()
        wait_send(halo_copies(c))
        if c >= chunks - SLOTS:
            wait_send(far_copies(c))
    for u in range(len(outs)):
        if u >= len(outs) - BUFFERS:
            sent(u)
        for m in mates:
            out_copy(u, m).wait_recv()


def decide(group, block, room, offsets, over):
    shape = (group, offsets.shape[1])
    rows = shape[1] // group
    slot = lax.broadcasted_iota(jnp.int32, shape, 1) - rows * lax.broadcasted_iota(jnp.int32, shape, 0)
    most = 0.0
    for n in lengths(offsets[...], block):
        n = jnp.broadcast_to(n.astype(jnp.float32), shape)
        most = jnp.maximum(most, jnp.sum(jnp.where((slot >= 0) & (slot < rows), n, 0.0), 1, keepdims=True))
    over[0] = (jnp.max(most) > room).astype(jnp.int32)


def choose(index, branches, *operands):
    traced = jax.make_jaxpr(lambda i, *args: lax.switch(i, branches, *args))(index, *operands)
    (switch,) = [eqn for eqn in traced.eqns if eqn.primitive.name == "cond"]
    assert list(switch.invars[1:]) == list(traced.jaxpr.invars[1:]) and not traced.consts
    return switch.primitive.bind(index, *operands, **switch.params)[0]


def body(frames, depth_offset, band_width, edge_level):
    group = lax.axis_size("scan") // LEAD
    local, all_rows, cols = frames.shape
    chunks, rows, block = cols // LANES, all_rows // group, local * group
    hi, spans = after(block), block // ROWS
    bins = -(-(block + 2 * DIFFUSE) // ROWS) * ROWS
    n_out = len(out_parts(chunks))
    dma = pltpu.SemaphoreType.DMA
    anywhere = pl.BlockSpec(memory_space=pl.ANY)

    def vmem(*shape):
        return pltpu.VMEM(shape, jnp.float32)

    def table(size):
        return pltpu.SMEM((size,), jnp.int32)

    def with_room(room, call):
        arrived = vmem(spans + room, ROWS, LANES)
        packed = vmem(SLOTS, room, ROWS, LANES)
        return pl.pallas_call(
            functools.partial(kernel, group, chunks, room),
            out_shape=jax.ShapeDtypeStruct(frames.shape, frames.dtype),
            in_specs=[anywhere] * 4,
            out_specs=anywhere,
            scratch_shapes=[arrived] * (2 * chunks)
            + [vmem((3 * block + LO + hi) * rows, LANES)] * SLOTS
            + [
                vmem(chunks, LO + block + hi + 2 * SWEEPS, rows, LANES),
                vmem(BUFFERS, block, rows, 2 * LANES),
                vmem(bins * rows, LANES),
                vmem(rows, LANES),
                packed,
                packed,
                pltpu.VMEM((rows, cols), jnp.int32),
            ]
            + [table(rows + 1)] * 6
            + [table(room)] * 2
            + [
                dma((chunks, group - 1)),
                dma((chunks, group - 1)),
                dma((chunks,)),
                dma((chunks, 2)),
                dma((chunks, 2)),
                dma((chunks, 2)),
                dma((chunks, 2)),
                dma((n_out, group - 1)),
                dma((n_out, group - 1)),
                dma((n_out,)),
                dma,
                table(all_rows),
                table(all_rows),
                dma((2,)),
            ],
            compiler_params=pltpu.CompilerParams(
                collective_id=call, has_side_effects=True, vmem_limit_bytes=54 * 1024 * 1024
            ),
        )

    whole = rows * spans
    half = whole // 2
    over = pl.pallas_call(
        functools.partial(decide, group, block, half),
        out_shape=pltpu.SMEM((1,), jnp.int32),
        in_specs=[pl.BlockSpec(memory_space=pltpu.VMEM)],
        out_specs=pl.BlockSpec(memory_space=pltpu.SMEM),
    )(depth_offset[None])
    kernels = [with_room(half, 0), with_room(whole, 1)]
    return choose(over.reshape(()), kernels, depth_offset, band_width, frames, edge_level)


def solution(mesh):
    placed = (P("scan", None, "col"), P(), P(), P(None, "col"))
    return jax.shard_map(
        body, mesh=mesh, in_specs=placed, out_specs=P("scan", None, "col"), check_vma=False
    )
```

```python
import functools

import jax
import jax.numpy as jnp
from jax import lax
from jax.experimental import pallas as pl
from jax.experimental.pallas import tpu as pltpu
from jax.sharding import PartitionSpec as P

SWEEPS = 6
DIFFUSE = 6
BAND = 8
STEP_SIZE = 0.24
LEVEL_SCALE = 16.0
LANES = 128
ROWS = 8
LEAD = 4
LAG = 1
SLOTS = 3
UNROLL = 8
LO = DIFFUSE + BAND - 1
MESH = pl.DeviceIdType.MESH
RATE = 1.0 / STEP_SIZE
UNIT = STEP_SIZE**0.5


def after(block):
    least = DIFFUSE + 1
    return least + -(LO + block + least) % ROWS


def lengths(offset, block):
    beyond = -offset + (DIFFUSE + 1 - after(block))
    up = (jnp.maximum(offset, 0) + ROWS - 1) // ROWS
    down = (jnp.maximum(beyond, 0) + ROWS - 1) // ROWS
    return up, down


def sweep_pass(load, store, n_in, n_out, sweeps, streams):
    lead = (n_in - n_out) // 2 + 2 * sweeps - 1

    def advance(t, carry):
        held, flux, made = carry
        at = jnp.minimum(t, n_in - 1)
        new_held, new_flux, new_made = [], [], []
        for s in range(streams):
            fresh = load(at, s)
            for level in range(sweeps):
                k = s * sweeps + level
                b = fresh if level == 0 else made[k - 1]
                a = held[k]
                c = b - a
                d = RATE + c * c
                q = pl.reciprocal(d, approx=True)
                f = c * (q * (2.0 - d * q))
                new_made.append(a + (f - flux[k]))
                new_held.append(b)
                new_flux.append(f)
        return tuple(new_held), tuple(new_flux), tuple(new_made)

    def work(t, carry):
        carry = advance(t + lead, carry)
        for s in range(streams):
            store(t, s, carry[2][s * sweeps + sweeps - 1])
        return carry

    start = tuple(load(0, s) for s in range(streams) for _ in range(sweeps))
    carry = lax.fori_loop(0, lead, advance, (start, start, start))
    lax.fori_loop(0, n_out, work, carry, unroll=UNROLL)


def kernel(group, chunks, room, offsets, widths, x, edge, out, *scratch):
    from_up = scratch[:chunks]
    from_down = scratch[chunks : 2 * chunks]
    wins = scratch[2 * chunks : 2 * chunks + SLOTS]
    (raw, made, prof, gain, pack_up, pack_down, edge_v, len_up, len_down, next_up, next_down, base_up, base_down,
     slot_up, slot_down, in_send, in_recv, in_own, halo_send, halo_recv, far_send, far_recv, out_send,
     out_recv, out_own, edge_sem, off_ref, bw_ref, table_sem) = scratch[2 * chunks + SLOTS :]
    local = x.shape[0]
    rows = x.shape[1] // group
    block = local * group
    hi = after(block)
    own_at = block + LO
    raw_at = LO + SWEEPS
    n_raw = raw.shape[1]
    ext = LO + block + hi
    spans = block // ROWS
    reach = 2 * block + ext
    me = lax.axis_index("scan")
    k = lax.rem(me, group)
    z = lax.div(me, group)
    tile_count = rows // ROWS
    pair = 2 if tile_count % 2 == 0 else 1

    def rows_of(j):
        return pl.ds(pl.multiple_of(j * rows, ROWS), rows)

    def cols_of(c):
        return pl.ds(c * LANES, LANES)

    mates = sorted(range(1, group), key=lambda m: -m.bit_count())

    def partner(m):
        at, bit = k, 1
        while bit < group:
            if m & bit:
                at = at + bit - 2 * bit * lax.rem(lax.div(k, bit), 2)
            bit *= 2
        return at

    def mate(m):
        return z * group + partner(m)

    has = {1: z < LEAD - 1, -1: z > 0}
    gets = {1: z > 0, -1: z < LEAD - 1}

    barrier = pltpu.get_barrier_semaphore()
    for m in mates:
        pl.semaphore_signal(barrier, inc=1, device_id={"scan": mate(m)}, device_id_type=MESH)
    for step in (1, -1):

        @pl.when(has[step])
        def _(step=step):
            pl.semaphore_signal(
                barrier, inc=1, device_id={"scan": me + step * group}, device_id_type=MESH
            )

    count = group - 1
    for step in (1, -1):
        count = count + has[step].astype(jnp.int32)
    pl.semaphore_wait(barrier, count)

    def in_copy(c, m):
        return pltpu.make_async_remote_copy(
            src_ref=x.at[:, rows_of(partner(m)), cols_of(c)],
            dst_ref=raw.at[c, pl.ds(raw_at + k * local, local)],
            send_sem=in_send.at[c, m - 1],
            recv_sem=in_recv.at[c, m - 1],
            device_id={"scan": mate(m)},
            device_id_type=MESH,
        )

    def in_local(c):
        return pltpu.make_async_copy(
            x.at[:, rows_of(k), cols_of(c)],
            raw.at[c, pl.ds(raw_at + k * local, local)],
            in_own.at[c],
        )

    def out_copy(c, m):
        return pltpu.make_async_remote_copy(
            src_ref=made.at[c % SLOTS, pl.ds(partner(m) * local, local)],
            dst_ref=out.at[:, rows_of(k), cols_of(c)],
            send_sem=out_send.at[c, m - 1],
            recv_sem=out_recv.at[c, m - 1],
            device_id={"scan": mate(m)},
            device_id_type=MESH,
        )

    def out_local(c):
        return pltpu.make_async_copy(
            made.at[c % SLOTS, pl.ds(k * local, local)],
            out.at[:, rows_of(k), cols_of(c)],
            out_own.at[c],
        )

    def z_copy(src, dst, sems, c, i, step):
        send, recv = sems
        return pltpu.make_async_remote_copy(
            src_ref=src,
            dst_ref=dst,
            send_sem=send.at[c, i],
            recv_sem=recv.at[c, i],
            device_id={"scan": me + step * group},
            device_id_type=MESH,
        )

    def halo_copies(c):
        sems = (halo_send, halo_recv)
        up = z_copy(
            raw.at[c, pl.ds(block, raw_at)], raw.at[c, pl.ds(0, raw_at)], sems, c, 0, 1
        )
        down = z_copy(
            raw.at[c, pl.ds(raw_at, hi + SWEEPS)],
            raw.at[c, pl.ds(raw_at + block, hi + SWEEPS)], sems, c, 1, -1,
        )
        return ((1, up), (-1, down))

    def far_copies(c):
        sems = (far_send, far_recv)
        up = z_copy(
            pack_up.at[c % SLOTS], from_up[c].at[pl.ds(spans, room)], sems, c, 0, 1
        )
        down = z_copy(
            pack_down.at[c % SLOTS], from_down[c].at[pl.ds(0, room)], sems, c, 1, -1
        )
        return ((1, up), (-1, down))

    def start(copies):
        for step, copy in copies:
            pl.when(has[step])(copy.start)

    def wait_recv(copies):
        for step, copy in copies:
            pl.when(gets[step])(copy.wait_recv)

    def wait_send(copies):
        for step, copy in copies:
            pl.when(has[step])(copy.wait_send)

    edge_copy = pltpu.make_async_copy(edge.at[rows_of(k)], edge_v, edge_sem)
    for c in range(chunks):
        for m in mates:
            in_copy(c, m).start()
        in_local(c).start()
    edge_copy.start()
    table_copies = [
        pltpu.make_async_copy(src, dst, table_sem.at[i])
        for i, (src, dst) in enumerate(((offsets, off_ref), (widths, bw_ref)))
    ]
    for copy in table_copies:
        copy.start()
    for copy in table_copies:
        copy.wait()

    for lens, nexts, bases in ((len_up, next_up, base_up), (len_down, next_down, base_down)):
        lens[rows] = jnp.int32(1)
        nexts[rows] = jnp.int32(rows)

    def measure(r, base):
        up, down = lengths(off_ref[k * rows + r], block)
        len_up[r], len_down[r] = up, down
        base_up[r], base_down[r] = base[0] + up, base[1]
        return base[0] + up, base[1] + down

    lax.fori_loop(0, rows, measure, (jnp.int32(0), jnp.int32(0)))

    def link(i, _):
        r = rows - 1 - i
        for lens, nexts in ((len_up, next_up), (len_down, next_down)):
            nexts[r] = jnp.where(lens[r + 1] > 0, r + 1, nexts[r + 1])
        return 0

    lax.fori_loop(0, rows, link, 0)

    def assign(j, carry):
        result = []
        lists = ((len_up, next_up, slot_up, own_at + block - LO), (len_down, next_down, slot_down, own_at + hi))
        for i, (lens, nexts, slots, first) in enumerate(lists):
            row, p = carry[2 * i], carry[2 * i + 1]
            n = lens[row]
            frame = first + ROWS * p - (ROWS * n if i == 0 else 0)
            slots[j] = jnp.where(row < rows, row * reach + frame, own_at)
            done = p + 1 >= n
            result.append(jnp.where(done, nexts[row], row))
            result.append(jnp.where(done, 0, p + 1))
        return tuple(result)

    heads = []
    for lens, nexts in ((len_up, next_up), (len_down, next_down)):
        heads.append(jnp.where(lens[0] > 0, 0, nexts[0]))
        heads.append(jnp.int32(0))
    lax.fori_loop(0, room, assign, tuple(heads))

    def arrive(c):
        in_local(c).wait()
        for m in mates:
            in_copy(c, m).wait_recv()
        start(halo_copies(c))

    def across(win, tile, frame):
        return win.at[pl.ds(tile * (ROWS * reach) + frame, ROWS, stride=reach)]

    def smooth(c):
        win = wins[c % SLOTS]
        wait_recv(halo_copies(c))

        @pl.when(z == 0)
        def _():
            for i in range(raw_at):
                raw[c, raw_at - 1 - i] = raw[c, raw_at + i]

        @pl.when(z == LEAD - 1)
        def _():
            for i in range(hi + SWEEPS):
                raw[c, raw_at + block + i] = raw[c, raw_at + block - 1 - i]

        def one(p, _):
            def load(t, s):
                at = pl.ds(pl.multiple_of((p * pair + s) * ROWS, ROWS), ROWS)
                return raw[c, t, at, :] * (1.0 / UNIT)

            def store(t, s, value):
                across(win, p * pair + s, block + t)[...] = value

            sweep_pass(load, store, n_raw, ext, SWEEPS, pair)
            return 0

        lax.fori_loop(0, tile_count // pair, one, 0)

        def repeat(first, number, source):
            values = [across(win, p, source)[...] for p in range(tile_count)]

            def one(i, _):
                for p in range(tile_count):
                    across(win, p, first + i)[...] = values[p]
                return 0

            lax.fori_loop(0, number, one, 0)

        pl.when(z == 0)(lambda: repeat(0, own_at, own_at))
        pl.when(z == LEAD - 1)(lambda: repeat(own_at + block, hi + block, own_at + block - 1))
        if c >= SLOTS:
            wait_send(far_copies(c - SLOTS))

        def pack(j, _):
            for slots, packed in ((slot_up, pack_up), (slot_down, pack_down)):
                packed[c % SLOTS, j] = win[pl.ds(slots[j], ROWS), :]
            return 0

        lax.fori_loop(0, room, pack, 0, unroll=4)
        start(far_copies(c))

    def unpack(win, source, bases, first):
        def one(r, _):
            base = bases[r]
            for m in range(spans):
                to = pl.multiple_of(r * reach + first + ROWS * m, ROWS)
                win[pl.ds(to, ROWS), :] = source[base + m]
            return 0

        lax.fori_loop(0, rows, one, 0)

    def depth(c):
        win = wins[c % SLOTS]
        wait_recv(far_copies(c))
        pl.when(gets[1])(lambda: unpack(win, from_up[c], base_up, 0))
        pl.when(gets[-1])(lambda: unpack(win, from_down[c], base_down, own_at + block + hi))

        for p in range(tile_count):
            tile = pl.ds(p * ROWS, ROWS)
            gain[tile, :] = LEVEL_SCALE / edge_v[tile, pl.ds(c * LANES, LANES)].astype(jnp.float32)

        def fill(r, _):
            width = bw_ref[k * rows + r]
            at_b = r * reach + own_at - DIFFUSE + 1 - off_ref[k * rows + r]
            at_a = at_b - width
            scale = jnp.broadcast_to(gain[pl.ds(r, 1), :], (ROWS, LANES)) / width.astype(jnp.float32)
            for m in range(prof.shape[0] // (rows * ROWS)):
                a = win[pl.ds(at_a + m * ROWS, ROWS), :]
                b = win[pl.ds(at_b + m * ROWS, ROWS), :]
                prof[pl.ds(m * ROWS * rows + r, ROWS, stride=rows), :] = (a - b) * scale
            return 0

        lax.fori_loop(0, rows, fill, 0)

        def bins(d):
            return pl.ds(d * rows, rows)

        @pl.when(z == 0)
        def _():
            for i in range(DIFFUSE):
                prof[bins(DIFFUSE - 1 - i), :] = prof[bins(DIFFUSE + i), :]

        @pl.when(z == LEAD - 1)
        def _():
            for i in range(DIFFUSE):
                prof[bins(DIFFUSE + block + i), :] = prof[bins(DIFFUSE + block - 1 - i), :]

        def one(p, _):
            tiles = [pl.ds(pl.multiple_of((p * pair + s) * ROWS, ROWS), ROWS) for s in range(pair)]
            scales = [
                edge_v[tile, pl.ds(c * LANES, LANES)].astype(jnp.float32) * (UNIT / LEVEL_SCALE) for tile in tiles
            ]

            def load(t, s):
                return prof[pl.ds(pl.multiple_of(t * rows + (p * pair + s) * ROWS, ROWS), ROWS), :]

            def store(t, s, value):
                made[c % SLOTS, t, tiles[s], :] = value * scales[s]

            sweep_pass(load, store, block + 2 * DIFFUSE, block, DIFFUSE, pair)
            return 0

        if c >= SLOTS:
            sent(c - SLOTS)
        lax.fori_loop(0, tile_count // pair, one, 0)
        for m in mates:
            out_copy(c, m).start()
        out_local(c).start()

    def sent(c):
        out_local(c).wait()
        for m in mates:
            out_copy(c, m).wait_send()

    arrive(0)
    for c in range(chunks):
        if c + 1 < chunks:
            arrive(c + 1)
        smooth(c)
        if c == 0:
            edge_copy.wait()
        if c >= LAG:
            depth(c - LAG)
    for c in range(max(chunks - LAG, 0), chunks):
        depth(c)
    for c in range(chunks):
        for m in mates:
            in_copy(c, m).wait_send()
        wait_send(halo_copies(c))
        if c >= chunks - SLOTS:
            wait_send(far_copies(c))
        if c >= chunks - SLOTS:
            sent(c)
        for m in mates:
            out_copy(c, m).wait_recv()


def decide(group, block, room, offsets, over):
    shape = (group, offsets.shape[1])
    rows = shape[1] // group
    slot = lax.broadcasted_iota(jnp.int32, shape, 1) - rows * lax.broadcasted_iota(jnp.int32, shape, 0)
    most = 0.0
    for n in lengths(offsets[...], block):
        n = jnp.broadcast_to(n.astype(jnp.float32), shape)
        most = jnp.maximum(most, jnp.sum(jnp.where((slot >= 0) & (slot < rows), n, 0.0), 1, keepdims=True))
    over[0] = (jnp.max(most) > room).astype(jnp.int32)


def choose(index, branches, *operands):
    traced = jax.make_jaxpr(lambda i, *args: lax.switch(i, branches, *args))(index, *operands)
    (switch,) = [eqn for eqn in traced.eqns if eqn.primitive.name == "cond"]
    assert list(switch.invars[1:]) == list(traced.jaxpr.invars[1:]) and not traced.consts
    return switch.primitive.bind(index, *operands, **switch.params)[0]


def body(frames, depth_offset, band_width, edge_level):
    group = lax.axis_size("scan") // LEAD
    local, all_rows, cols = frames.shape
    chunks, rows, block = cols // LANES, all_rows // group, local * group
    hi, spans = after(block), block // ROWS
    bins = -(-(block + 2 * DIFFUSE) // ROWS) * ROWS
    dma = pltpu.SemaphoreType.DMA
    anywhere = pl.BlockSpec(memory_space=pl.ANY)

    def vmem(*shape):
        return pltpu.VMEM(shape, jnp.float32)

    def table(size):
        return pltpu.SMEM((size,), jnp.int32)

    def with_room(room, call):
        arrived = vmem(spans + room, ROWS, LANES)
        packed = vmem(SLOTS, room, ROWS, LANES)
        return pl.pallas_call(
            functools.partial(kernel, group, chunks, room),
            out_shape=jax.ShapeDtypeStruct(frames.shape, frames.dtype),
            in_specs=[anywhere] * 4,
            out_specs=anywhere,
            scratch_shapes=[arrived] * (2 * chunks)
            + [vmem((3 * block + LO + hi) * rows, LANES)] * SLOTS
            + [
                vmem(chunks, LO + block + hi + 2 * SWEEPS, rows, LANES),
                vmem(SLOTS, block, rows, LANES),
                vmem(bins * rows, LANES),
                vmem(rows, LANES),
                packed,
                packed,
                pltpu.VMEM((rows, cols), jnp.int32),
            ]
            + [table(rows + 1)] * 6
            + [table(room)] * 2
            + [
                dma((chunks, group - 1)),
                dma((chunks, group - 1)),
                dma((chunks,)),
                dma((chunks, 2)),
                dma((chunks, 2)),
                dma((chunks, 2)),
                dma((chunks, 2)),
                dma((chunks, group - 1)),
                dma((chunks, group - 1)),
                dma((chunks,)),
                dma,
                table(all_rows),
                table(all_rows),
                dma((2,)),
            ],
            compiler_params=pltpu.CompilerParams(
                collective_id=call, has_side_effects=True, vmem_limit_bytes=52 * 1024 * 1024
            ),
        )

    whole = rows * spans
    half = whole // 2
    over = pl.pallas_call(
        functools.partial(decide, group, block, half),
        out_shape=pltpu.SMEM((1,), jnp.int32),
        in_specs=[pl.BlockSpec(memory_space=pltpu.VMEM)],
        out_specs=pl.BlockSpec(memory_space=pltpu.SMEM),
    )(depth_offset[None])
    kernels = [with_room(half, 0), with_room(whole, 1)]
    return choose(over.reshape(()), kernels, depth_offset, band_width, frames, edge_level)


def solution(mesh):
    placed = (P("scan", None, "col"), P(), P(), P(None, "col"))
    return jax.shard_map(
        body, mesh=mesh, in_specs=placed, out_specs=P("scan", None, "col"), check_vma=False
    )
```
